32 devices in a mesh: dp: 8 (over z, y), seq: 4 (over x, core).
Axes of the slice: x: 2, y: 2, z: 4, core: 2. Of those that a mesh axis runs over, the one named last changes fastest.
Arguments:
- block_input: bfloat16 [16, 1024, 1024], P('dp', 'seq'), may hold values from -6 to 6
- doc_ids: int32 [16, 1024], P('dp'), may hold values from 0 to 5, never falling along the last dimension, each value on 1 to 512 neighbouring positions
- gain_attn: float32 [1024], P(('dp', 'seq')), may hold values from 0.25 to 1.75
- shift_attn: float32 [1024], P(('dp', 'seq')), may hold values from -4 to 4
- w_qkv: float32 [1024, 3072], P(('dp', 'seq')), may hold values from -0.1875 to 0.1875
- bias_qv: float32 [2048], P(('dp', 'seq')), may hold values from -6 to 6
- w_proj: float32 [1024, 1024], P(('dp', 'seq')), may hold values from -6 to 6
- bias_proj: float32 [1024], P(('dp', 'seq')), may hold values from -6 to 6
- gain_mlp: float32 [1024], P(('dp', 'seq')), may hold values from 0.25 to 1.75
- shift_mlp: float32 [1024], P(('dp', 'seq')), may hold values from -4 to 4
- w_up: float32 [1024, 4096], P(('dp', 'seq')), may hold values from -0.1875 to 0.1875
- bias_up: float32 [4096], P(('dp', 'seq')), may hold values from -6 to 6
- w_down: float32 [4096, 1024], P(('dp', 'seq')), may hold values from -0.875 to 0.875
- bias_down: float32 [1024], P(('dp', 'seq')), may hold values from -6 to 6
- out_grad: bfloat16 [16, 1024, 1024], P('dp', 'seq'), may hold values from -6 to 6
Outputs:
- block_out: bfloat16 [16, 1024, 1024], P('dp', 'seq')
- grad_input: float32 [16, 1024, 1024], P('dp', 'seq')
- d_gain_attn: float32 [1024], P(('dp', 'seq'))
- d_shift_attn: float32 [1024], P(('dp', 'seq'))
- d_w_qkv: float32 [1024, 3072], P(('dp', 'seq'))
- d_bias_qv: float32 [2048], P(('dp', 'seq'))
- d_w_proj: float32 [1024, 1024], P(('dp', 'seq'))
- d_bias_proj: float32 [1024], P(('dp', 'seq'))
- d_gain_mlp: float32 [1024], P(('dp', 'seq'))
- d_shift_mlp: float32 [1024], P(('dp', 'seq'))
- d_w_up: float32 [1024, 4096], P(('dp', 'seq'))
- d_bias_up: float32 [4096], P(('dp', 'seq'))
- d_w_down: float32 [4096, 1024], P(('dp', 'seq'))
- d_bias_down: float32 [1024], P(('dp', 'seq'))
The draws below stay inside these ranges and needn't reach their ends.
Inputs may be any that keep to these rules, and one draw needn't show every extreme that they name: `doc_ids`: in each row the document numbers never fall; every one of the 6 documents has 1 to 512 tokens.
All inputs are finite; a program needn't handle non-finite values.
Results may differ from the reference program's by a relative error of at most 0.012.
The reference program's roundings to bfloat16 on the way count: a program that leaves them out, or rounds other values in their place, can miss the bound.
Values may be sent and summed in bfloat16 or wider, within the bound.
No kernel may reach another device: no remote copies, remote signals or barrier semaphores. Data moves between devices by JAX's collectives and lax.ppermute only.
A program may use at most 256 MiB of HBM per device.

```python
import math
import jax
import jax.numpy as jnp
import numpy as np
from jax import lax

D = 1024
H = 16
HD = 64
FF = 4096
LAYERS = 24
LEN = 1024
DOCS = 6
ROWS_DEV = 2
ROWS = 16


def levels(stream_key, extent, pieces, smallest, high):
    loudness, own = 1.0, jax.random.fold_in(stream_key, 6)
    for dim, blocks in pieces:
        draws = jnp.exp(jax.random.uniform(jax.random.fold_in(own, dim), (blocks,), jnp.float32, smallest / len(pieces), high / len(pieces)))
        loudness = loudness * jnp.repeat(draws, extent[dim] // blocks).reshape([-1 if axis == dim else 1 for axis in range(len(extent))])
    return loudness


def length_profile(number_of, total, limit, skew):
    weights = [(1 << 20) // math.isqrt(rank ** skew) + 1 for rank in range(2, number_of + 1)]
    rest, holding = total - limit - (number_of - 1), [1] * (number_of - 1)
    while rest > 0:
        candidates = [i for i in range(number_of - 1) if holding[i] < limit]
        whole, left = sum([weights[i] for i in candidates]), rest
        for i in candidates:
            extra = min(limit - holding[i], max(1, left * weights[i] // whole), rest)
            holding[i] = holding[i] + extra
            rest = rest - extra
    return np.array([limit] + holding)


def uneven(rng, number_of, total, limit, lean):
    if number_of == 2:
        one = jax.random.randint(rng, (), max(1, total - limit), min(limit, total - 1) + 1)
        return jnp.stack([one, total - one])
    tallies = jnp.asarray(length_profile(number_of, total, limit, lean), jnp.int32)
    couples = (number_of - 1) // 2
    source_of, taker = tallies[1:1 + 2 * couples:2], tallies[2:2 + 2 * couples:2]
    slack = jnp.minimum(source_of - 1, limit - taker)
    moved = jax.random.randint(jax.random.fold_in(rng, 1), (couples,), 0, 1 << 20) % (slack + 1)
    tallies = tallies.at[1:1 + 2 * couples:2].set(source_of - moved).at[2:2 + 2 * couples:2].set(taker + moved)
    return tallies[jax.random.permutation(jax.random.fold_in(rng, 2), number_of)]


def normal_values(key, shape, scale, bound, shards=(), kind=jnp.bfloat16):
    values = jax.random.normal(key, shape, jnp.float32) * scale
    if len(shards) > 0:
        values = levels(key, shape, shards, -0.22, 0.18) * values
    return jnp.clip(values, min=-bound, max=bound).astype(kind)


def setup_inputs(seed: int = 0) -> dict:
    streams_of = jax.random.split(jax.random.key(seed), 16)
    block_input = normal_values(streams_of[0], (ROWS, LEN, D), 1.0, 6.0, ((0, 8), (1, 4)))
    doc_ids = jax.vmap(lambda own: jnp.searchsorted(jnp.cumsum(uneven(own, DOCS, LEN, LEN // 2, 2)), jnp.arange(LEN), side="right"))(jax.random.split(streams_of[1], ROWS)).reshape((ROWS, LEN)).astype(jnp.int32)
    gain_attn = jnp.clip(1.0 + 0.15 * jax.random.normal(streams_of[2], (D,), jnp.float32), 0.25, 1.75)
    shift_attn = normal_values(streams_of[3], (D,), 0.3, 4.0, ((0, 32),), jnp.float32)
    w_qkv = normal_values(streams_of[4], (D, 3 * D), D ** -0.5, 0.1875, ((0, 32),), jnp.float32)
    bias_qv = normal_values(streams_of[5], (2 * D,), 0.5, 6.0, ((0, 32),), jnp.float32)
    w_proj = normal_values(streams_of[6], (D, D), 0.5, 6.0, ((0, 32),), jnp.float32)
    bias_proj = normal_values(streams_of[7], (D,), 1.0, 6.0, ((0, 32),), jnp.float32)
    gain_mlp = jnp.clip(1.0 + 0.15 * jax.random.normal(streams_of[8], (D,), jnp.float32), 0.25, 1.75)
    shift_mlp = normal_values(streams_of[9], (D,), 0.3, 4.0, ((0, 32),), jnp.float32)
    w_up = normal_values(streams_of[10], (D, FF), D ** -0.5, 0.1875, ((0, 32),), jnp.float32)
    bias_up = normal_values(streams_of[11], (FF,), 0.5, 6.0, ((0, 32),), jnp.float32)
    w_down = normal_values(streams_of[12], (FF, D), 0.06, 0.875, ((0, 32),), jnp.float32)
    bias_down = normal_values(streams_of[13], (D,), 1.0, 6.0, ((0, 32),), jnp.float32)
    out_grad = normal_values(streams_of[14], (ROWS, LEN, D), 1.0, 6.0, ((0, 8), (1, 4)))
    return dict(block_input=block_input, doc_ids=doc_ids, gain_attn=gain_attn, shift_attn=shift_attn, w_qkv=w_qkv, bias_qv=bias_qv, w_proj=w_proj, bias_proj=bias_proj, gain_mlp=gain_mlp, shift_mlp=shift_mlp, w_up=w_up, bias_up=bias_up, w_down=w_down, bias_down=bias_down, out_grad=out_grad)


@jax.custom_vjp
def low(v):
    return lax.optimization_barrier(v.astype(jnp.bfloat16)).astype(jnp.float32)

@jax.custom_vjp
def low_back(v):
    return v

def low_keep(v):
    return (low(v), None)

def low_pass(kept, grad):
    return (grad,)

def back_keep(v):
    return (v, None)

def back_low(kept, grad):
    return (low(grad),)
low.defvjp(low_keep, low_pass)
low_back.defvjp(back_keep, back_low)
EPSILON = 1e-05
HIGHEST = lax.Precision.HIGHEST

def layer_norm(values, gain, shift):
    mean = lax.optimization_barrier(jnp.mean(values, axis=-1, keepdims=True))
    centred = values - mean
    spread = lax.optimization_barrier(jnp.mean(centred * centred, axis=-1, keepdims=True))
    return centred * lax.rsqrt(spread + EPSILON) * gain + shift

def forward(inputs, doc_rows, params):
    gain_attn, shift_attn, w_qkv, bias_qv, w_proj, bias_proj, gain_mlp, shift_mlp, w_up, bias_up, w_down, bias_down = [low(param) for param in params]
    rows = inputs.shape[0]
    depth = LAYERS ** (-0.5)
    normed = low(layer_norm(inputs, gain_attn, shift_attn))
    bias_full = jnp.concatenate([bias_qv[:D], jnp.zeros((D,), jnp.float32), bias_qv[D:]])
    mixed = jnp.einsum('rtd,de->rte', normed, w_qkv, precision=HIGHEST) + bias_full
    mixed = low(low_back(mixed)).reshape(rows, LEN, 3, H, HD)
    raw = jnp.einsum('rqhd,rkhd->rhqk', mixed[:, :, 0], mixed[:, :, 1], precision=HIGHEST)
    scores = low_back(raw * HD ** (-0.5))
    places = jnp.arange(LEN, dtype=jnp.int32)
    causal = places[:, None] >= places[None, :]
    allowed = (doc_rows[:, :, None] == doc_rows[:, None, :]) & causal[None]
    scores = jnp.where(allowed[:, None], scores, -1e+30)
    attn_probs = low(jax.nn.softmax(scores, axis=-1))
    attended = jnp.einsum('rhqk,rkhd->rqhd', attn_probs, mixed[:, :, 2], precision=HIGHEST)
    attended = low(low_back(attended.reshape(rows, LEN, D)))
    branch = low_back(jnp.einsum('rtd,de->rte', attended, w_proj, precision=HIGHEST) + bias_proj)
    hidden = inputs + depth * branch
    normed_mlp = low(layer_norm(hidden, gain_mlp, shift_mlp))
    upward = low_back(jnp.einsum('rtd,df->rtf', normed_mlp, w_up, precision=HIGHEST) + bias_up)
    active = low(jax.nn.gelu(upward, approximate=True))
    lowered = low_back(jnp.einsum('rtf,fd->rtd', active, w_down, precision=HIGHEST) + bias_down)
    return hidden + depth * lowered

def reference(block_input, doc_ids, gain_attn, shift_attn, w_qkv, bias_qv, w_proj, bias_proj, gain_mlp, shift_mlp, w_up, bias_up, w_down, bias_down, out_grad):
    params = (gain_attn, shift_attn, w_qkv, bias_qv, w_proj, bias_proj, gain_mlp, shift_mlp, w_up, bias_up, w_down, bias_down)
    groups = ROWS // ROWS_DEV
    inputs = block_input.astype(jnp.float32).reshape(groups, ROWS_DEV, LEN, D)
    doc_groups = doc_ids.reshape(groups, ROWS_DEV, LEN)
    cotangents = out_grad.astype(jnp.float32).reshape(groups, ROWS_DEV, LEN, D)

    def one_group(totals, item):
        group_in, group_docs, group_cot = item

        def apply(values, *weights):
            return forward(values, group_docs, weights)
        result, pull = jax.vjp(apply, group_in, *params)
        grads = pull(group_cot)
        totals = tuple((total + grad for total, grad in zip(totals, grads[1:])))
        return (totals, (result.astype(jnp.bfloat16), grads[0]))
    start = tuple((jnp.zeros_like(param) for param in params))
    totals, (results, grad_in) = lax.scan(one_group, start, (inputs, doc_groups, cotangents))
    return (results.reshape(ROWS, LEN, D), grad_in.reshape(ROWS, LEN, D), totals[0], totals[1], totals[2], totals[3], totals[4], totals[5], totals[6], totals[7], totals[8], totals[9], totals[10], totals[11])
```

```python
import jax
import jax.numpy as jnp
from jax import lax
from jax.experimental import pallas as pl
from jax.experimental.pallas import tpu as pltpu
from jax.sharding import Mesh, PartitionSpec as P

H = 16
LAYERS = 24
EPSILON = 1e-05
DOC_MAX = 512

BF = jnp.bfloat16
F32 = jnp.float32


def half(values):
    return values.astype(BF)


def norm_parts(values):
    mean = jnp.mean(values, axis=-1, keepdims=True)
    centred = values - mean
    spread = jnp.mean(centred * centred, axis=-1, keepdims=True)
    inverse = lax.rsqrt(spread + EPSILON)
    return (centred * inverse, inverse)


def norm_back(grad_out, normal, inverse, gain):
    scaled = grad_out * gain
    return inverse * (
        scaled
        - jnp.mean(scaled, axis=-1, keepdims=True)
        - normal * jnp.mean(scaled * normal, axis=-1, keepdims=True)
    )


def dot(left, right, contract):
    return lax.dot_general(left, right, ((contract[:1], contract[1:]), ((), ())), preferred_element_type=F32)


def shift(value, axis, step):
    size = lax.axis_size(axis)
    return lax.ppermute(value, axis, [(i, (i + step) % size) for i in range(size)])


def in_order(parts, axis):
    size = len(parts)
    here = lax.axis_index(axis)
    return [lax.select_n(lax.rem(here - place + size, size), *parts) for place in range(size)]


def gather_axis(value, axis, at):
    size = lax.axis_size(axis)
    parts = [value] + [shift(value, axis, k) for k in range(1, size)]
    return jnp.stack(in_order(parts, axis), axis=at)


def swap_axis(value, axis, at):
    size = lax.axis_size(axis)
    here = lax.axis_index(axis)
    parts = []
    for k in range(size):
        block = lax.dynamic_index_in_dim(value, lax.rem(here + k, size), at, keepdims=False)
        parts.append(shift(block, axis, k) if k else block)
    return in_order(parts, axis)


def reduce_axis(value, axis, at):
    size = lax.axis_size(axis)
    here = lax.axis_index(axis)
    total = lax.dynamic_index_in_dim(value, here, at, keepdims=False).astype(F32)
    for k in range(1, size):
        block = lax.dynamic_index_in_dim(value, lax.rem(here + k, size), at, keepdims=False)
        total = total + shift(half(block), axis, k).astype(F32)
    return total


def gather_pair(first, second):
    rows = first.shape[0]
    both = gather_axis(jnp.concatenate([first, second], axis=0), "z", 0)
    first, second = both[:, :rows], both[:, rows:]
    first = gather_axis(gather_axis(first, "g", 1), "y", 1)
    second = gather_axis(gather_axis(second, "y", 1), "g", 2)
    return first, second


def reduce_pair(first, second):
    rows = first.shape[3]
    first = half(reduce_axis(first, "g", 2))
    second = half(reduce_axis(second, "y", 1))
    first = reduce_axis(first, "y", 1)
    second = reduce_axis(second, "g", 1)
    both = reduce_axis(jnp.concatenate([first, second], axis=1), "z", 0)
    return both[:rows], both[rows:]


def spans(length, block):
    for start in range(0, length, block):
        low = max(0, start - DOC_MAX)
        yield start, low, start + block - low


def hidden_part(docs_q, docs_k, start, low, block, width):
    key_pos = low + lax.broadcasted_iota(jnp.int32, (width, block), 0)
    query_pos = start + lax.broadcasted_iota(jnp.int32, (width, block), 1)
    return (docs_k == docs_q) & (key_pos <= query_pos)


def attend_kernel(block, head_dim, q_ref, k_ref, v_ref, docs_row_ref, docs_col_ref, out_ref, log_ref):
    length, lanes = q_ref.shape
    heads = lanes // head_dim
    v_t = v_ref[...].T
    for start, low, width in spans(length, block):
        visible = hidden_part(
            docs_row_ref[:, start : start + block], docs_col_ref[low : low + width], start, low, block, width
        )
        q = q_ref[start : start + block] * (head_dim ** (-0.5))
        lane = lax.broadcasted_iota(jnp.int32, q.shape, 1) // head_dim
        outs = []
        for head in range(heads):
            q_head = jnp.where(lane == head, q, jnp.zeros_like(q))
            scores = dot(k_ref[low : low + width], q_head, (1, 1))
            scores = jnp.where(visible, scores, -1e30)
            top = jnp.max(scores, axis=0, keepdims=True)
            exponent = jnp.exp(scores - top)
            total = jnp.sum(exponent, axis=0, keepdims=True)
            probs = half(exponent * (1.0 / total))
            outs.append(dot(v_t[head * head_dim : (head + 1) * head_dim, low : low + width], probs, (1, 0)))
            log_ref[0, head : head + 1, start : start + block] = top + jnp.log(total)
        out_ref[start : start + block] = half(jnp.concatenate(outs, axis=0).T)


def attend_back_kernel(
    block, head_dim, q_ref, k_ref, v_ref, g_ref, log_ref, docs_row_ref, docs_col_ref, dq_ref, dk_ref, dv_ref, key_sum, value_sum
):
    length, lanes = q_ref.shape
    heads = lanes // head_dim
    scale = head_dim ** (-0.5)
    k_t = k_ref[...].T
    key_sum[...] = jnp.zeros_like(key_sum)
    value_sum[...] = jnp.zeros_like(value_sum)
    for start, low, width in spans(length, block):
        visible = hidden_part(
            docs_row_ref[:, start : start + block], docs_col_ref[low : low + width], start, low, block, width
        )
        q = q_ref[start : start + block] * scale
        g = g_ref[start : start + block]
        lane = lax.broadcasted_iota(jnp.int32, q.shape, 1) // head_dim
        dq, dk, dv = [], 0.0, 0.0
        for head in range(heads):
            q_head = jnp.where(lane == head, q, jnp.zeros_like(q))
            g_head = jnp.where(lane == head, g, jnp.zeros_like(g))
            scores = dot(k_ref[low : low + width], q_head, (1, 1))
            scores = jnp.where(visible, scores, -1e30)
            probs = jnp.exp(scores - log_ref[0, head : head + 1, start : start + block])
            grad_probs = dot(v_ref[low : low + width], g_head, (1, 1))
            delta = jnp.sum(grad_probs * probs, axis=0, keepdims=True)
            grad_scores = half(probs * (grad_probs - delta))
            dq.append(dot(k_t[head * head_dim : (head + 1) * head_dim, low : low + width], grad_scores, (1, 0)))
            dk = dk + dot(grad_scores, q_head, (1, 0))
            dv = dv + dot(half(probs), g_head, (1, 0))
        dq_ref[start : start + block] = half((jnp.concatenate(dq, axis=0) * scale).T)
        key_sum[low : low + width] += dk
        value_sum[low : low + width] += dv
    dk_ref[...] = half(key_sum[...])
    dv_ref[...] = half(value_sum[...])


def attend_specs(length, lanes, steps):
    def column(offset):
        return pl.BlockSpec((length, lanes), lambda i: (0, offset * steps + i))

    whole_row = pl.BlockSpec((1, length), lambda i: (0, 0))
    whole_col = pl.BlockSpec((length, 1), lambda i: (0, 0))
    return column, whole_row, whole_col


def attend(qk, value, docs, head_dim):
    length, width = value.shape
    block = min(256, length)
    lanes = min(128, width)
    steps = width // lanes
    column, whole_row, whole_col = attend_specs(length, lanes, steps)
    logs = pl.BlockSpec((1, lanes // head_dim, length), lambda i: (i, 0, 0))

    def kernel(*refs):
        attend_kernel(block, head_dim, *refs)

    return pl.pallas_call(
        kernel,
        grid=(steps,),
        in_specs=[column(0), column(1), column(0), whole_row, whole_col],
        out_specs=[column(0), logs],
        out_shape=[
            jax.ShapeDtypeStruct((length, width), BF),
            jax.ShapeDtypeStruct((steps, lanes // head_dim, length), F32),
        ],
        compiler_params=pltpu.CompilerParams(vmem_limit_bytes=48 << 20),
        name="attend",
    )(qk, qk, value, docs[None], docs[:, None])


def attend_back(qk, value, grad_out, logs, docs, head_dim):
    length, width = value.shape
    block = min(256, length)
    lanes = min(128, width)
    steps = width // lanes
    column, whole_row, whole_col = attend_specs(length, lanes, steps)
    logs_spec = pl.BlockSpec((1, lanes // head_dim, length), lambda i: (i, 0, 0))

    def kernel(*refs):
        attend_back_kernel(block, head_dim, *refs)

    shape = jax.ShapeDtypeStruct((length, width), BF)
    return pl.pallas_call(
        kernel,
        grid=(steps,),
        in_specs=[column(0), column(1), column(0), column(0), logs_spec, whole_row, whole_col],
        out_specs=[column(0), column(0), column(0)],
        out_shape=[shape, shape, shape],
        scratch_shapes=[pltpu.VMEM((length, lanes), F32), pltpu.VMEM((length, lanes), F32)],
        compiler_params=pltpu.CompilerParams(vmem_limit_bytes=48 << 20),
        name="attend_back",
    )(qk, qk, value, grad_out, logs, docs[None], docs[:, None])


def gelu_parts(u):
    c = 0.7978845608028654
    inner = jnp.tanh(c * (u + 0.044715 * (u * u * u)))
    value = 0.5 * u * (1.0 + inner)
    slope = 0.5 * (1.0 + inner) + 0.5 * u * (1.0 - inner * inner) * (c * (1.0 + 3 * 0.044715 * (u * u)))
    return value, slope


def body(
    block_input,
    doc_ids,
    gain_attn,
    shift_attn,
    w_qkv,
    bias_qv,
    w_proj,
    bias_proj,
    gain_mlp,
    shift_mlp,
    w_up,
    bias_up,
    w_down,
    bias_down,
    out_grad,
):
    zs, ys, gs, ts = (lax.axis_size(a) for a in ("z", "y", "g", "t"))
    blocks = zs * ys * gs
    t = lax.axis_index("t")
    g = lax.axis_index("g")
    depth = LAYERS ** (-0.5)
    rows, local, width = block_input.shape
    length = doc_ids.shape[1]
    shard = w_qkv.shape[0]
    part = width // ts
    head_dim = width // H
    hidden_width = w_up.shape[1]
    ff_shard = w_down.shape[0]
    ff_half = ff_shard // 2
    ff_part = hidden_width // ts // 2
    own = gs * local

    docs = lax.dynamic_index_in_dim(doc_ids, g, 0, keepdims=False)

    x_own = jnp.stack(swap_axis(block_input, "g", 0), axis=0)
    x_all = gather_axis(x_own, "t", 1).reshape(length, width)
    grad_own = jnp.stack(swap_axis(out_grad, "g", 0), axis=0).astype(F32)
    grad_down_own = half(depth * grad_own)
    grad_down = gather_axis(grad_down_own, "t", 1).reshape(length, width)

    vectors = [gain_attn, shift_attn, bias_qv, bias_proj, gain_mlp, shift_mlp, bias_up, bias_down]
    sizes = [v.shape[0] for v in vectors]
    packed = half(jnp.concatenate(vectors))
    count = packed.shape[0]
    w_q, w_k, w_v = (w.reshape(shard, ts, part) for w in jnp.split(half(w_qkv), 3, axis=1))
    w_o = half(w_proj).reshape(shard, ts, part)
    w_u = half(w_up).reshape(shard, blocks, ts, 2, ff_half)
    w_u = [w_u[:, :, :, i].transpose(0, 2, 1, 3).reshape(shard, ts, ff_part) for i in range(2)]
    columns = jnp.concatenate([w_q, w_k, w_v, w_o, *w_u], axis=2)
    columns = jnp.concatenate(swap_axis(columns, "t", 1), axis=0)
    packed_all = jnp.concatenate([gather_axis(packed, "t", 0).reshape(-1), jnp.zeros((2 * part - ts * count,), BF)])
    extra = 8
    shard_qk = jnp.concatenate(
        [columns[:, : 2 * part], jnp.broadcast_to(packed_all[None], (extra, 2 * part))], axis=0
    )
    shard_vo = columns[:, 2 * part : 4 * part]
    shard_u1 = columns[:, 4 * part : 4 * part + ff_part]
    shard_u2 = columns[:, 4 * part + ff_part :]
    shard_d = half(w_down)

    full_qk, full_vo = gather_pair(shard_qk, shard_vo)
    full_u1, full_u2 = gather_pair(shard_u1, shard_u2)
    full_d1, full_d2 = gather_pair(shard_d[:ff_half], shard_d[ff_half:])

    vector_rows = full_qk[:, :, :, ts * shard, : ts * count].reshape(blocks, ts, count)
    offsets = [0]
    for size in sizes:
        offsets.append(offsets[-1] + size)
    pieces = [vector_rows[:, :, offsets[i] : offsets[i + 1]] for i in range(len(sizes))]
    h_gain_attn, h_shift_attn, h_bias_qv, h_bias_proj, h_gain_mlp, h_shift_mlp = (
        p.reshape(-1).astype(F32) for p in pieces[:6]
    )
    h_bias_down = pieces[7].reshape(-1).astype(F32)
    h_bias_up = lax.dynamic_index_in_dim(pieces[6], t, 1, keepdims=False).astype(F32)
    h_bias_up = h_bias_up.reshape(blocks, 2, ff_half)
    h_bias_up = [h_bias_up[:, i].reshape(-1) for i in range(2)]
    bias_q = lax.dynamic_slice_in_dim(h_bias_qv, t * part, part)
    bias_v = lax.dynamic_slice_in_dim(h_bias_qv, width + t * part, part)
    wqk = full_qk[:, :, :, : ts * shard].reshape(width, 2 * part)
    wvo = full_vo.reshape(width, 2 * part)
    wv = wvo[:, :part]
    wo = jnp.concatenate(
        in_order(
            [wvo[:, part:]] + [shift(wvo[:, part:], "t", k) for k in range(1, ts)],
            "t",
        ),
        axis=1,
    )
    wu = [full_u1.reshape(width, ff_part), full_u2.reshape(width, ff_part)]
    wd = [full_d1.reshape(ff_part, width), full_d2.reshape(ff_part, width)]

    normal_all, _ = norm_parts(x_all.astype(F32))
    normed_attn = half(normal_all * h_gain_attn + h_shift_attn)
    qk = half(dot(normed_attn, wqk, (1, 0)) + jnp.concatenate([bias_q, jnp.zeros((part,), F32)]))
    value = half(dot(normed_attn, wv, (1, 0)) + bias_v)
    attended_heads, logs = attend(qk, value, docs, head_dim)
    attended = jnp.concatenate(swap_axis(attended_heads.reshape(gs, ts, local, part), "t", 1), axis=-1)
    attended = attended.reshape(own, width)
    x_flat = x_own.reshape(own, width).astype(F32)
    hidden = x_flat + depth * (dot(attended, wo, (1, 0)) + h_bias_proj)
    normal_two, inverse_two = norm_parts(hidden)
    normed_own = half(normal_two * h_gain_mlp + h_shift_mlp)
    normed_mlp = gather_axis(normed_own.reshape(gs, local, width), "t", 1).reshape(length, width)
    lowered = 0.0
    grad_up, d_down, d_bias_up = [], [], []
    actives, slopes = [], []
    for i in range(2):
        upward = dot(normed_mlp, wu[i], (1, 0)) + h_bias_up[i]
        active, slope = gelu_parts(upward)
        active = half(active)
        actives.append(active)
        slopes.append(slope)
        d_down.append(half(dot(active, grad_down, (0, 0))).reshape(zs, ys, gs, ff_half, width))
    sum_d1, sum_d2 = reduce_pair(*d_down)
    for i in range(2):
        grad_up.append(half(dot(grad_down, wd[i], (1, 1)) * slopes[i]))
        d_bias_up.append(jnp.sum(grad_up[i], axis=0, dtype=F32))
    d_up = [half(dot(normed_mlp, grad_up[i], (0, 0))).reshape(zs, ys, gs, ts * shard, ff_part) for i in range(2)]
    sum_u = reduce_pair(*d_up)
    e2 = dot(grad_up[0], wu[0], (1, 1)) + dot(grad_up[1], wu[1], (1, 1))
    e2 = reduce_axis(e2.reshape(gs, ts, local, width), "t", 1).reshape(own, width)
    lowered = dot(actives[0], wd[0], (1, 0)) + dot(actives[1], wd[1], (1, 0))
    lowered = reduce_axis(lowered.reshape(gs, ts, local, width), "t", 1).reshape(own, width)
    block_out = half(hidden + depth * (lowered + h_bias_down)).reshape(gs, local, width)
    block_out = jnp.stack(swap_axis(block_out, "g", 0), axis=0)

    d_gain_mlp = jnp.sum(e2 * normal_two, axis=0)
    d_shift_mlp = jnp.sum(e2, axis=0)
    grad_hidden = grad_own.reshape(own, width) + norm_back(e2, normal_two, inverse_two, h_gain_mlp)
    grad_branch = half(depth * grad_hidden)
    d_bias_proj = jnp.sum(grad_branch, axis=0, dtype=F32)
    d_proj = dot(attended, grad_branch, (0, 0))
    d_proj = reduce_axis(d_proj.reshape(width, ts, part), "t", 1)
    grad_attended = half(dot(grad_branch, wo, (1, 1))).reshape(own, ts, part)
    grad_attended = jnp.stack(
        [p.reshape(gs, local, part) for p in swap_axis(grad_attended, "t", 1)], axis=1
    ).reshape(length, part)
    dq, dk, dv = attend_back(qk, value, grad_attended, logs, docs, head_dim)
    d_qk = jnp.concatenate([dq, dk], axis=1)
    e1 = dot(d_qk, wqk, (1, 1)) + dot(dv, wv, (1, 1))
    e1 = reduce_axis(e1.reshape(gs, ts, local, width), "t", 1).reshape(own, width)
    normal_one, inverse_one = norm_parts(x_flat)
    d_gain_attn = jnp.sum(e1 * normal_one, axis=0)
    d_shift_attn = jnp.sum(e1, axis=0)
    grad_input = grad_hidden + norm_back(e1, normal_one, inverse_one, h_gain_attn)
    grad_input = half(grad_input).reshape(gs, local, width)
    grad_input = jnp.stack(swap_axis(grad_input, "g", 0), axis=0).astype(F32)

    def by_owner(full):
        return full.reshape(blocks, ts, -1)

    d_bias_q = jnp.sum(dq, axis=0, dtype=F32)
    d_bias_v = jnp.sum(dv, axis=0, dtype=F32)
    d_bias_qv = jnp.zeros((2 * width,), F32)
    d_bias_qv = lax.dynamic_update_slice_in_dim(d_bias_qv, d_bias_q, t * part, 0)
    d_bias_qv = lax.dynamic_update_slice_in_dim(d_bias_qv, d_bias_v, width + t * part, 0)
    d_bias_up = jnp.stack([d.reshape(blocks, ff_half) for d in d_bias_up], axis=1).reshape(blocks, 1, ff_shard)
    d_bias_up = jnp.where(lax.broadcasted_iota(jnp.int32, (blocks, ts, 1), 1) == t, d_bias_up, 0.0)
    d_bias_down = jnp.sum(grad_down_own, axis=(0, 1), dtype=F32)
    vector_sums = jnp.concatenate(
        [
            by_owner(d_gain_attn),
            by_owner(d_shift_attn),
            by_owner(d_bias_qv),
            by_owner(d_bias_proj),
            by_owner(d_gain_mlp),
            by_owner(d_shift_mlp),
            d_bias_up,
            by_owner(d_bias_down),
        ],
        axis=2,
    )
    vector_sums = reduce_axis(vector_sums, "t", 1)
    vector_sums = jnp.pad(half(vector_sums), ((0, 0), (0, 2 * part - count)))
    vector_sums = jnp.broadcast_to(vector_sums[:, None], (blocks, extra, 2 * part))
    d_wqk = half(dot(normed_attn, d_qk, (0, 0))).reshape(blocks, ts * shard, 2 * part)
    d_wqk = jnp.concatenate([d_wqk, vector_sums], axis=1).reshape(zs, ys, gs, ts * shard + extra, 2 * part)
    d_wv = half(dot(normed_attn, dv, (0, 0)))
    d_wvo = jnp.concatenate([d_wv, half(d_proj)], axis=1).reshape(zs, ys, gs, ts * shard, 2 * part)
    sum_qk, sum_vo = reduce_pair(d_wqk, d_wvo)
    vector_sums = sum_qk[ts * shard, :count]
    out_vectors = [vector_sums[offsets[i] : offsets[i + 1]] for i in range(len(sizes))]

    up = jnp.stack(sum_u, axis=0).reshape(2, ts, shard, blocks, ff_half)
    up = jnp.stack(swap_axis(up, "t", 1), axis=0)
    sum_up = up.transpose(2, 3, 0, 1, 4).reshape(shard, hidden_width)
    rest = jnp.concatenate([sum_qk[: ts * shard], sum_vo], axis=1).reshape(ts, shard, 4, part)
    rest = jnp.stack(swap_axis(rest, "t", 0), axis=2)
    sum_qkv = rest[:, :3].reshape(shard, 3 * width)
    sum_proj = rest[:, 3].reshape(shard, width)
    sum_down = jnp.concatenate([sum_d1, sum_d2], axis=0)
    return (
        block_out,
        grad_input,
        out_vectors[0],
        out_vectors[1],
        sum_qkv,
        out_vectors[2],
        sum_proj,
        out_vectors[3],
        out_vectors[4],
        out_vectors[5],
        sum_up,
        out_vectors[6],
        sum_down,
        out_vectors[7],
    )


def solution(mesh):
    rows = 2
    dp, seq = mesh.shape["dp"], mesh.shape["seq"]
    high = 4
    split = Mesh(mesh.devices.reshape(high, dp // high, rows, seq // rows), ("z", "y", "g", "t"))
    everything = ("z", "y", "g", "t")
    tokens = P(("z", "y"), ("g", "t"), None)
    vector = P(everything)
    matrix = P(everything, None)
    return jax.shard_map(
        body,
        mesh=split,
        in_specs=(
            tokens,
            P(("z", "y"), None),
            vector,
            vector,
            matrix,
            vector,
            matrix,
            vector,
            vector,
            vector,
            matrix,
            vector,
            matrix,
            vector,
            tokens,
        ),
        out_specs=(
            tokens,
            tokens,
            vector,
            vector,
            matrix,
            vector,
            matrix,
            vector,
            vector,
            vector,
            matrix,
            vector,
            matrix,
            vector,
        ),
        check_vma=False,
    )
```

```python
import jax
import jax.numpy as jnp
from jax import lax
from jax.experimental import pallas as pl
from jax.experimental.pallas import tpu as pltpu
from jax.sharding import Mesh, PartitionSpec as P

H = 16
LAYERS = 24
EPSILON = 1e-05
DOC_MAX = 512

BF = jnp.bfloat16
F32 = jnp.float32


def half(values):
    return values.astype(BF)


def norm_parts(values):
    mean = jnp.mean(values, axis=-1, keepdims=True)
    centred = values - mean
    spread = jnp.mean(centred * centred, axis=-1, keepdims=True)
    inverse = lax.rsqrt(spread + EPSILON)
    return (centred * inverse, inverse)


def norm_back(grad_out, normal, inverse, gain):
    scaled = grad_out * gain
    return inverse * (
        scaled
        - jnp.mean(scaled, axis=-1, keepdims=True)
        - normal * jnp.mean(scaled * normal, axis=-1, keepdims=True)
    )


def dot(left, right, contract):
    return lax.dot_general(left, right, ((contract[:1], contract[1:]), ((), ())), preferred_element_type=F32)


def cost(microseconds):
    return pl.CostEstimate(flops=int(microseconds * 9e8), bytes_accessed=int(microseconds * 3e6), transcendentals=0)


def after(value, *others):
    return lax.optimization_barrier((value, *others))[0]


def shift(value, axis, step):
    size = lax.axis_size(axis)
    return lax.ppermute(value, axis, [(i, (i + step) % size) for i in range(size)])


def gather_relative(value, axis):
    return [value] + [shift(value, axis, k) for k in range(1, lax.axis_size(axis))]


def return_relative(blocks, axis):
    return [blocks[0]] + [shift(block, axis, -k) for k, block in enumerate(blocks) if k]


def by_place(parts, axis, sign):
    size = len(parts)
    here = lax.axis_index(axis)
    return [lax.select_n(lax.rem(sign * (place - here) + size, size), *parts) for place in range(size)]


def swap_axis(value, axis, at):
    size = lax.axis_size(axis)
    here = lax.axis_index(axis)
    parts = []
    for k in range(size):
        block = lax.dynamic_index_in_dim(value, lax.rem(here + k, size), at, keepdims=False)
        parts.append(shift(block, axis, k) if k else block)
    return by_place(parts, axis, -1)


def reduce_axis(value, axis, at):
    size = lax.axis_size(axis)
    here = lax.axis_index(axis)
    total = lax.dynamic_index_in_dim(value, here, at, keepdims=False)
    for k in range(1, size):
        block = lax.dynamic_index_in_dim(value, lax.rem(here + k, size), at, keepdims=False)
        total = total + shift(block, axis, k)
    return total


def whole(memory_space=pltpu.VMEM):
    return pl.BlockSpec(memory_space=memory_space)


def assemble(place, firsts, seconds, wanted, shapes):
    ny, ng = len(firsts), len(seconds)
    nz, high, wide = firsts[0].shape[1:]

    def kernel(place_ref, *refs):
        ins, outs = (refs[:ny], refs[ny : ny + ng]), refs[ny + ng :]
        y, g = place_ref[1], place_ref[2]
        for pieces, out in zip(wanted, outs):
            for which, row, rows, column, columns, into in pieces:
                for ky in range(ny):
                    for kg in range(ng):
                        source = ins[0][ky].at[kg, 0] if which == 0 else ins[1][kg].at[ky, 0]
                        at = (0, lax.rem(y - ky + ny, ny), lax.rem(g - kg + ng, ng))
                        out[(*at, slice(None), pl.ds(into, columns))] = source[row : row + rows, column : column + columns]

    def out_spec(shape):
        return pl.BlockSpec((1, ny, ng, *shape), lambda i, place_ref: (lax.rem(place_ref[0] - i + nz, nz), 0, 0, 0, 0))

    return pl.pallas_call(
        kernel,
        grid_spec=pltpu.PrefetchScalarGridSpec(
            num_scalar_prefetch=1,
            grid=(nz,),
            in_specs=[pl.BlockSpec((ng, 1, high, wide), lambda i, place_ref: (0, i, 0, 0))] * ny
            + [pl.BlockSpec((ny, 1, high, wide), lambda i, place_ref: (0, i, 0, 0))] * ng,
            out_specs=[out_spec(shape) for shape in shapes],
        ),
        out_shape=[jax.ShapeDtypeStruct((nz, ny, ng, *shape), BF) for shape in shapes],
        compiler_params=pltpu.CompilerParams(vmem_limit_bytes=16 << 20),
        cost_estimate=cost(4),
        name="assemble",
    )(place, *firsts, *seconds)


def gather_over_z(shard):
    parts = gather_relative(shard, "z")
    middle = shard.shape[1] // 2
    return jnp.stack([p[:, :middle] for p in parts]), jnp.stack([p[:, middle:] for p in parts])


def gather_once(first, second):
    return jnp.stack(gather_relative(first, "g")), jnp.stack(gather_relative(second, "y"))


def gather_twice(first, second):
    return gather_relative(first, "y"), gather_relative(second, "g")


def weight_grad_kernel(sizes, place_ref, left_ref, right_ref, *refs):
    nz, ny, ng = sizes
    middle = (len(refs) - 1) - (ny + ng)
    kept, outs, total = refs[:middle], refs[middle:-1], refs[-1]
    y, g = place_ref[1], place_ref[2]
    width = right_ref.shape[1]
    total[:, :width] = dot(left_ref[...], right_ref[...], (0, 0))
    if kept:
        total[:, width:] = kept[0][...].astype(F32)
    columns = total.shape[1] // 2
    rows = total.shape[0] // (ny * ng)
    for k in range(ng):
        at = lax.rem(g + k, ng)
        for i in range(ny):
            start = pl.multiple_of((i * ng + at) * rows, rows)
            outs[k][0, i] = half(total[pl.ds(start, rows), :columns])
    for k in range(ny):
        at = lax.rem(y + k, ny)
        for i in range(ng):
            start = pl.multiple_of((at * ng + i) * rows, rows)
            outs[ng + k][0, i] = half(total[pl.ds(start, rows), columns:])


def weight_grad(place, sizes, left, right, more=None):
    nz, ny, ng = sizes
    tokens, height = left.shape
    width = right.shape[1] + (more.shape[1] if more is not None else 0)
    rows, columns = height // (nz * ny * ng), width // 2

    def kernel(*refs):
        weight_grad_kernel(sizes, *refs)

    first = jax.ShapeDtypeStruct((nz, ny, rows, columns), BF)
    second = jax.ShapeDtypeStruct((nz, ng, rows, columns), BF)
    step = height // nz
    extra = [] if more is None else [more]
    outs = pl.pallas_call(
        kernel,
        grid=(nz,),
        in_specs=[
            whole(pltpu.SMEM),
            pl.BlockSpec((tokens, step), lambda i: (0, i)),
            pl.BlockSpec((tokens, right.shape[1]), lambda i: (0, 0)),
        ]
        + [pl.BlockSpec((step, m.shape[1]), lambda i: (i, 0)) for m in extra],
        out_specs=[pl.BlockSpec((1, ny, rows, columns), lambda i: (i, 0, 0, 0))] * ng
        + [pl.BlockSpec((1, ng, rows, columns), lambda i: (i, 0, 0, 0))] * ny,
        out_shape=[first] * ng + [second] * ny,
        scratch_shapes=[pltpu.VMEM((step, width), F32)],
        compiler_params=pltpu.CompilerParams(vmem_limit_bytes=20 << 20),
        cost_estimate=cost(7),
        name="weight_grad",
    )(place, left, right, *extra)
    return outs[:ng], outs[ng:]


def total_of(refs, at):
    value = refs[0][at].astype(F32)
    for ref in refs[1:]:
        value = value + ref[at].astype(F32)
    return value


def add_split(place, sizes, first, second):
    nz, ny, ng = sizes
    rows, columns = first[0].shape[2:]

    def kernel(place_ref, *refs):
        firsts, seconds, outs = refs[:ng], refs[ng : ng + ny], refs[ng + ny :]
        y, g = place_ref[1], place_ref[2]
        for k in range(ny):
            outs[k][0] = half(total_of(firsts, (0, lax.rem(y + k, ny))))
        for k in range(ng):
            outs[ny + k][0] = half(total_of(seconds, (0, lax.rem(g + k, ng))))

    shape = jax.ShapeDtypeStruct((nz, rows, columns), BF)
    outs = pl.pallas_call(
        kernel,
        grid=(nz,),
        in_specs=[whole(pltpu.SMEM)]
        + [pl.BlockSpec((1, ny, rows, columns), lambda i: (i, 0, 0, 0))] * ng
        + [pl.BlockSpec((1, ng, rows, columns), lambda i: (i, 0, 0, 0))] * ny,
        out_specs=[pl.BlockSpec((1, rows, columns), lambda i: (i, 0, 0))] * (ny + ng),
        out_shape=[shape] * (ny + ng),
        compiler_params=pltpu.CompilerParams(vmem_limit_bytes=12 << 20),
        cost_estimate=cost(3.5),
        name="add_split",
    )(place, *first, *second)
    return outs[:ny], outs[ny:]


def split_over_z(place, first, second):
    ny, ng = len(first), len(second)
    nz, rows, columns = first[0].shape

    def kernel(place_ref, *refs):
        firsts, seconds, outs = refs[:ny], refs[ny : ny + ng], refs[ny + ng :]
        z = place_ref[0]
        for k in range(nz):
            at = lax.rem(z + k, nz)
            outs[k][:, :columns] = total_of(firsts, at).astype(outs[k].dtype)
            outs[k][:, columns:] = total_of(seconds, at).astype(outs[k].dtype)

    return pl.pallas_call(
        kernel,
        in_specs=[whole(pltpu.SMEM)] + [whole()] * (ny + ng),
        out_specs=[whole()] * nz,
        out_shape=[jax.ShapeDtypeStruct((rows, 2 * columns), BF if k else F32) for k in range(nz)],
        compiler_params=pltpu.CompilerParams(vmem_limit_bytes=12 << 20),
        cost_estimate=cost(2.5),
        name="split_over_z",
    )(place, *first, *second)


def send_parts(first, second, axis_first, axis_second):
    first = [first[0]] + [shift(b, axis_first, k) for k, b in enumerate(first) if k]
    second = [second[0]] + [shift(b, axis_second, k) for k, b in enumerate(second) if k]
    return first, second


def reduce_in_layer(place, sizes, parts, *others):
    first, second = parts
    first = [after(first[0], *others)] + first[1:]
    return send_parts(*add_split(place, sizes, first, second), "y", "g")


def reduce_over_z(place, parts, *others):
    first, second = parts
    first = [after(first[0], *others)] + first[1:]
    blocks = split_over_z(place, first, second)
    return [blocks[0]] + [shift(block, "z", k) for k, block in enumerate(blocks) if k]


def total_sum(blocks):
    total = blocks[0]
    for block in blocks[1:]:
        total = total + block.astype(F32)
    return total


def key_blocks(start, block):
    return range(max(0, start - DOC_MAX), start + block, block)


def visible_part(first_ref, low, start, block, rows, row):
    key_pos = low + row + lax.broadcasted_iota(jnp.int32, (rows, block), 0)
    visible = key_pos >= first_ref[:, start : start + block]
    if low == start:
        visible &= key_pos <= start + lax.broadcasted_iota(jnp.int32, (rows, block), 1)
    return visible


def fold(values, op):
    rows, lanes = values.shape
    return op(values.reshape(rows // 8, 8, lanes), axis=0)


def for_heads(values, head_dim):
    lane = lax.broadcasted_iota(jnp.int32, values.shape, 1) // head_dim
    heads = values.shape[1] // head_dim
    return jnp.concatenate([jnp.where(lane == h, values, jnp.zeros_like(values)) for h in range(heads)], axis=0)


def heads_of(values, head_dim, block):
    heads = values.shape[0] // head_dim
    return jnp.concatenate(
        [values[h * head_dim : (h + 1) * head_dim, h * block : (h + 1) * block] for h in range(heads)], axis=0
    )


def load_in_order(order_ref, source, into, local, columns):
    for n in range(into.shape[0] // local):
        rows = pl.ds(pl.multiple_of(order_ref[n] * local, local), local)
        into[n * local : (n + 1) * local] = source[rows, columns]


def store_in_order(order_ref, source, into, local, columns):
    for n in range(source.shape[0] // local):
        rows = pl.ds(pl.multiple_of(order_ref[n] * local, local), local)
        into[rows, columns] = half(source[n * local : (n + 1) * local])


def attend_kernel(block, sub, head_dim, local, order_ref, qkv_ref, first_ref, out_ref, log_ref, q_s, k_s, v_s, o_s, s_s):
    length, lanes = q_s.shape
    heads = lanes // head_dim
    for i, into in enumerate((q_s, k_s, v_s)):
        load_in_order(order_ref, qkv_ref, into, local, slice(i * lanes, (i + 1) * lanes))
    v_t = v_s[...].T
    for start in range(0, length, block):
        q_heads = for_heads(q_s[start : start + block] * (head_dim ** (-0.5)), head_dim)
        lows = list(key_blocks(start, block))
        top8 = [jnp.full((8, block), -1e30, F32)] * heads
        for n, low in enumerate(lows):
            scores = dot(k_s[low : low + block], q_heads, (1, 1))
            for r in range(0, block, sub):
                visible = visible_part(first_ref, low, start, block, sub, r)
                rows = slice(n * block + r, n * block + r + sub)
                for h in range(heads):
                    columns = slice(h * block, (h + 1) * block)
                    piece = jnp.where(visible, scores[r : r + sub, columns], -1e30)
                    top8[h] = jnp.maximum(top8[h], fold(piece, jnp.max))
                    s_s[rows, columns] = piece
        width = len(lows) * block
        top = jnp.concatenate([jnp.max(v, axis=0, keepdims=True) for v in top8], axis=1)
        total8 = jnp.zeros((8, heads * block), F32)
        for r in range(0, width, sub):
            exponent = jnp.exp(s_s[r : r + sub] - top)
            total8 = total8 + fold(exponent, jnp.sum)
            s_s[r : r + sub] = exponent
        total = jnp.sum(total8, axis=0, keepdims=True)
        probs = half(s_s[:width] * (1.0 / total))
        out = dot(v_t[:, lows[0] : lows[0] + width], probs, (1, 0))
        log = top + jnp.log(total)
        for h in range(heads):
            log_ref[0, h : h + 1, start : start + block] = log[:, h * block : (h + 1) * block]
        o_s[start : start + block] = half(heads_of(out, head_dim, block).T)
    store_in_order(order_ref, o_s, out_ref, local, slice(None))


def attend_back_kernel(
    block,
    sub,
    head_dim,
    local,
    order_ref,
    qkv_ref,
    g_ref,
    log_ref,
    first_ref,
    out_ref,
    q_s,
    k_s,
    v_s,
    g_s,
    query_grad,
    key_sum,
    value_sum,
    p_s,
    d_s,
):
    length, lanes = q_s.shape
    heads = lanes // head_dim
    scale = head_dim ** (-0.5)
    for i, into in enumerate((q_s, k_s, v_s)):
        load_in_order(order_ref, qkv_ref, into, local, slice(i * lanes, (i + 1) * lanes))
    load_in_order(order_ref, g_ref, g_s, local, slice(None))
    k_t = k_s[...].T
    for start in range(0, length, block):
        q_heads = for_heads(q_s[start : start + block] * scale, head_dim)
        g_heads = for_heads(g_s[start : start + block], head_dim)
        lows = list(key_blocks(start, block))
        delta8 = [jnp.zeros((8, block), F32)] * heads
        for n, low in enumerate(lows):
            scores = dot(k_s[low : low + block], q_heads, (1, 1))
            grads = dot(v_s[low : low + block], g_heads, (1, 1))
            for r in range(0, block, sub):
                visible = visible_part(first_ref, low, start, block, sub, r)
                rows = slice(n * block + r, n * block + r + sub)
                for h in range(heads):
                    columns = slice(h * block, (h + 1) * block)
                    p = jnp.where(visible, scores[r : r + sub, columns], -1e30)
                    p = jnp.exp(p - log_ref[0, h : h + 1, start : start + block])
                    d = grads[r : r + sub, columns]
                    delta8[h] = delta8[h] + fold(p * d, jnp.sum)
                    p_s[rows, columns] = p
                    d_s[rows, columns] = d
        delta = jnp.concatenate([jnp.sum(v, axis=0, keepdims=True) for v in delta8], axis=1)
        width = len(lows) * block
        p = p_s[:width]
        grad_scores = half(p * (d_s[:width] - delta))
        dq = dot(k_t[:, lows[0] : lows[0] + width], grad_scores, (1, 0))
        dk = dot(grad_scores, q_heads, (1, 0))
        dv = dot(half(p), g_heads, (1, 0))
        for n, low in enumerate(lows):
            rows = slice(n * block, (n + 1) * block)
            if low == start:
                key_sum[low : low + block] = dk[rows]
                value_sum[low : low + block] = dv[rows]
            else:
                key_sum[low : low + block] += dk[rows]
                value_sum[low : low + block] += dv[rows]
        query_grad[start : start + block] = (heads_of(dq, head_dim, block) * scale).T
    for i, source in enumerate((query_grad, key_sum, value_sum)):
        store_in_order(order_ref, source, out_ref, local, slice(i * lanes, (i + 1) * lanes))


def attend(qkv, first, order, local, head_dim):
    length, width = qkv.shape
    block = min(256, length)
    window = min(length, DOC_MAX + block)
    lanes = 2 * head_dim
    steps = width // (3 * lanes)

    def kernel(*refs):
        attend_kernel(block, 64, head_dim, local, *refs)

    return pl.pallas_call(
        kernel,
        grid=(steps,),
        in_specs=[
            whole(pltpu.SMEM),
            pl.BlockSpec((length, 3 * lanes), lambda i: (0, i)),
            pl.BlockSpec((1, length), lambda i: (0, 0)),
        ],
        out_specs=[
            pl.BlockSpec((length, lanes), lambda i: (0, i)),
            pl.BlockSpec((1, 2, length), lambda i: (i, 0, 0)),
        ],
        out_shape=[
            jax.ShapeDtypeStruct((length, width // 3), BF),
            jax.ShapeDtypeStruct((steps, 2, length), F32),
        ],
        scratch_shapes=[pltpu.VMEM((length, lanes), BF)] * 4 + [pltpu.VMEM((window, 2 * block), F32)],
        compiler_params=pltpu.CompilerParams(vmem_limit_bytes=16 << 20),
        cost_estimate=cost(11.5 * steps / 4),
        name="attend",
    )(order, qkv, first[None])


def attend_back(qkv, grad_out, logs, first, order, local, head_dim):
    length, width = qkv.shape
    block = min(256, length)
    window = min(length, DOC_MAX + block)
    lanes = 2 * head_dim
    steps = width // (3 * lanes)

    def kernel(*refs):
        attend_back_kernel(block, 64, head_dim, local, *refs)

    return pl.pallas_call(
        kernel,
        grid=(steps,),
        in_specs=[
            whole(pltpu.SMEM),
            pl.BlockSpec((length, 3 * lanes), lambda i: (0, i)),
            pl.BlockSpec((length, lanes), lambda i: (0, i)),
            pl.BlockSpec((1, 2, length), lambda i: (i, 0, 0)),
            pl.BlockSpec((1, length), lambda i: (0, 0)),
        ],
        out_specs=pl.BlockSpec((length, 3 * lanes), lambda i: (0, i)),
        out_shape=jax.ShapeDtypeStruct((length, width), BF),
        scratch_shapes=[pltpu.VMEM((length, lanes), BF)] * 4
        + [pltpu.VMEM((length, lanes), F32)] * 3
        + [pltpu.VMEM((window, 2 * block), F32)] * 2,
        compiler_params=pltpu.CompilerParams(vmem_limit_bytes=20 << 20),
        cost_estimate=cost(18 * steps / 4),
        name="attend_back",
    )(order, qkv, grad_out, logs, first[None])


def gelu_parts(u):
    c = 0.7978845608028654
    square = u * u
    h = 0.5 + 0.5 * jnp.tanh(u * (c + (c * 0.044715) * square))
    value = u * h
    return value, h + value * (1.0 - h) * (2 * c + (6 * c * 0.044715) * square)


def up_part(normed, weight, bias):
    tokens, width = normed.shape
    ff = weight.shape[1]
    block = min(256, ff)
    rows = min(256, tokens)

    def kernel(x_ref, w_ref, b_ref, active_ref, slope_ref):
        for r in range(0, tokens, rows):
            u = dot(x_ref[r : r + rows], w_ref[...], (1, 0)) + b_ref[...]
            value, slope = gelu_parts(u)
            active_ref[r : r + rows] = half(value)
            slope_ref[r : r + rows] = slope

    column = pl.BlockSpec((tokens, block), lambda i: (0, i))
    return pl.pallas_call(
        kernel,
        grid=(ff // block,),
        in_specs=[
            pl.BlockSpec((tokens, width), lambda i: (0, 0)),
            pl.BlockSpec((width, block), lambda i: (0, i)),
            pl.BlockSpec((1, block), lambda i: (0, i)),
        ],
        out_specs=[column, column],
        out_shape=[jax.ShapeDtypeStruct((tokens, ff), BF), jax.ShapeDtypeStruct((tokens, ff), F32)],
        compiler_params=pltpu.CompilerParams(vmem_limit_bytes=16 << 20),
        cost_estimate=cost(7),
        name="up_part",
    )(normed, weight, bias[None])


def up_back(grad_down, weight, slope):
    tokens, width = grad_down.shape
    ff = weight.shape[0]
    block = min(256, ff)
    rows = min(256, tokens)

    def kernel(g_ref, w_ref, slope_ref, out_ref, sum_ref):
        total = jnp.zeros((8, block), F32)
        for r in range(0, tokens, rows):
            grad = half(dot(g_ref[r : r + rows], w_ref[...], (1, 1)) * slope_ref[r : r + rows])
            out_ref[r : r + rows] = grad
            total = total + fold(grad.astype(F32), jnp.sum)
        sum_ref[...] = jnp.sum(total, axis=0, keepdims=True)

    column = pl.BlockSpec((tokens, block), lambda i: (0, i))
    return pl.pallas_call(
        kernel,
        grid=(ff // block,),
        in_specs=[
            pl.BlockSpec((tokens, width), lambda i: (0, 0)),
            pl.BlockSpec((block, width), lambda i: (i, 0)),
            column,
        ],
        out_specs=[column, pl.BlockSpec((1, block), lambda i: (0, i))],
        out_shape=[jax.ShapeDtypeStruct((tokens, ff), BF), jax.ShapeDtypeStruct((1, ff), F32)],
        compiler_params=pltpu.CompilerParams(vmem_limit_bytes=16 << 20),
        cost_estimate=cost(6.5),
        name="up_back",
    )(grad_down, weight, slope)


def body(
    block_input,
    doc_ids,
    gain_attn,
    shift_attn,
    w_qkv,
    bias_qv,
    w_proj,
    bias_proj,
    gain_mlp,
    shift_mlp,
    w_up,
    bias_up,
    w_down,
    bias_down,
    out_grad,
):
    nz, ny, ng, nt = (lax.axis_size(a) for a in ("z", "y", "g", "t"))
    sizes = (nz, ny, ng)
    z, y, g, t = (lax.axis_index(a) for a in ("z", "y", "g", "t"))
    place = jnp.stack([z, y, g]).astype(jnp.int32)
    chips = nz * ny * ng
    depth = LAYERS ** (-0.5)
    _, local, width = block_input.shape
    length = doc_ids.shape[1]
    shard = w_qkv.shape[0]
    part = width // nt
    head_dim = width // H
    lanes = 2 * head_dim
    pairs = part // lanes
    hidden_width = w_up.shape[1]
    ff_shard = w_down.shape[0]
    ff_part = hidden_width // nt
    own = ng * local
    block_rows = nt * shard

    natural = jnp.arange(ng * nt, dtype=jnp.int32)
    order = lax.rem(t - natural % nt + nt, nt) * ng + lax.rem(g - natural // nt + ng, ng)
    docs = lax.dynamic_index_in_dim(doc_ids, g, 0, keepdims=False)
    first_token = jnp.sum((docs[None, :] < docs[:, None]).astype(jnp.int32), axis=1)

    both = jnp.stack([block_input, out_grad], axis=1)
    parts = []
    for k in range(ng):
        block = lax.dynamic_index_in_dim(both, lax.rem(g + k, ng), 0, keepdims=False)
        parts.append(shift(block, "g", k) if k else block)
    both_own = jnp.concatenate(parts, axis=1)
    x_own, grad_own = both_own[0].astype(F32), both_own[1].astype(F32)
    both_all = jnp.concatenate(gather_relative(both_own, "t"), axis=1)

    vectors = [gain_attn, shift_attn, bias_qv, bias_proj, gain_mlp, shift_mlp, bias_up, bias_down]
    counts = [v.shape[0] for v in vectors]
    packed = half(lax.optimization_barrier(jnp.concatenate(vectors)))
    count = packed.shape[0]
    columns_a = half(w_qkv).reshape(shard, 3, nt, pairs, lanes).transpose(2, 0, 3, 1, 4).reshape(nt, shard, 3 * part)
    columns_o = half(w_proj).reshape(shard, nt, part).transpose(1, 0, 2)
    columns_u = half(w_up).reshape(shard, chips, nt, ff_shard).transpose(2, 0, 1, 3).reshape(nt, shard, ff_part)
    columns = jnp.concatenate([columns_a, columns_o, columns_u], axis=2)
    wide = columns.shape[2]
    packed = jnp.broadcast_to(jnp.pad(packed, (0, wide - count)), (nt, 8, wide))
    columns = swap_axis(jnp.concatenate([columns, packed], axis=1), "t", 0)
    packed = jnp.concatenate([c[shard : shard + 1, :count] for c in columns], axis=1)
    columns = jnp.concatenate([c[:shard] for c in columns], axis=0)
    packed = jnp.broadcast_to(jnp.pad(packed, ((0, 0), (0, 4 * part - nt * count))), (8, 4 * part))
    shard_a = jnp.concatenate([columns[:, : 4 * part], packed], axis=0)
    shard_u = columns[:, 4 * part :]
    shard_d = half(w_down)
    middle_d = width // 2

    first_a, second_a = gather_over_z(shard_a)
    first_d, second_d = gather_once(shard_d[:, :middle_d], shard_d[:, middle_d:])
    first_u, second_u = gather_over_z(after(shard_u, first_a, second_a))
    first_a, second_a = gather_once(first_a, second_a)
    first_a, second_a = gather_twice(first_a, second_a)
    side = 3 * part - 2 * part
    wqkv, wo, vector_rows = assemble(
        place,
        first_a,
        second_a,
        [
            [(0, 0, block_rows, 0, 2 * part, 0), (1, 0, block_rows, 0, side, 2 * part)],
            [(1, 0, block_rows, side, part, 0)],
            [(0, block_rows, 8, 0, 2 * part, 0)],
        ],
        [(block_rows, 3 * part), (block_rows, part), (8, 2 * part)],
    )
    wqkv = wqkv.reshape(width, 3 * part)
    wo = wo.reshape(width, part)
    first_u, second_u = gather_once(after(first_u, *first_a, *second_a), after(second_u, *first_a, *second_a))

    vector_rows = vector_rows.reshape(chips, 8, 2 * part)[:, 0, : nt * count].reshape(chips, nt, count)
    offsets = [0]
    for size in counts:
        offsets.append(offsets[-1] + size)
    pieces = [vector_rows[:, :, offsets[i] : offsets[i + 1]] for i in range(len(counts))]
    h_gain_attn, h_shift_attn, h_bias_qv, h_bias_proj, h_gain_mlp, h_shift_mlp = (
        p.reshape(-1).astype(F32) for p in pieces[:6]
    )
    h_bias_down = pieces[7].reshape(-1).astype(F32)
    h_bias_up = lax.dynamic_index_in_dim(pieces[6], t, 1, keepdims=False).astype(F32).reshape(-1)
    bias_q = lax.dynamic_slice_in_dim(h_bias_qv, t * part, part).reshape(pairs, lanes)
    bias_v = lax.dynamic_slice_in_dim(h_bias_qv, width + t * part, part).reshape(pairs, lanes)
    bias_qkv = jnp.stack([bias_q, jnp.zeros_like(bias_q), bias_v], axis=1).reshape(-1)

    normal_all, _ = norm_parts(both_all[0].astype(F32))
    normed_attn = half(normal_all * h_gain_attn + h_shift_attn)
    grad_down = half(depth * both_all[1].astype(F32))
    qkv = half(dot(normed_attn, wqkv, (1, 0)) + bias_qkv)
    both_d = gather_relative(after(jnp.concatenate([first_d, second_d], axis=0), first_u), "z")
    attended_heads, logs = attend(qkv, first_token, order, local, head_dim)
    first_u, second_u = gather_twice(first_u, second_u)
    wo = jnp.concatenate(by_place(gather_relative(wo, "t"), "t", -1), axis=1)
    attended = return_relative([attended_heads[k * own : (k + 1) * own] for k in range(nt)], "t")
    attended = jnp.concatenate(by_place(attended, "t", 1), axis=1)
    hidden = x_own + depth * (dot(attended, wo, (1, 0)) + h_bias_proj)
    normal_two, inverse_two = norm_parts(hidden)
    normed_own = half(normal_two * h_gain_mlp + h_shift_mlp)
    normed_mlp = jnp.concatenate(gather_relative(normed_own, "t"), axis=0)
    (wu,) = assemble(
        place,
        first_u,
        second_u,
        [[(0, 0, block_rows, 0, ff_part // 2, 0), (1, 0, block_rows, 0, ff_part // 2, ff_part // 2)]],
        [(block_rows, ff_part)],
    )
    wu = wu.reshape(width, ff_part)
    first_d = jnp.stack([b[:ng] for b in both_d], axis=1)
    second_d = jnp.stack([b[ng:] for b in both_d], axis=1)
    first_d, second_d = gather_twice(after(first_d, *first_u, *second_u), after(second_d, *first_u, *second_u))
    active, slope = up_part(normed_mlp, wu, h_bias_up)

    def own_sum(left, right):
        blocks = [half(dot(left[k * own : (k + 1) * own], right, (1, 1))) for k in range(1, nt)]
        mine = dot(after(left[:own], *blocks), right, (1, 1))
        return total_sum([mine] + [shift(block, "t", -k - 1) for k, block in enumerate(blocks)])

    down_parts = send_parts(*weight_grad(place, sizes, active, grad_down), "g", "y")
    (wd,) = assemble(
        place,
        first_d,
        second_d,
        [[(0, 0, ff_shard, 0, middle_d, 0), (1, 0, ff_shard, 0, middle_d, middle_d)]],
        [(ff_shard, width)],
    )
    wd = wd.reshape(ff_part, width)
    grad_up, d_bias_up = up_back(grad_down, wd, slope)
    up_blocks = weight_grad(place, sizes, normed_mlp, grad_up)
    down_parts = reduce_in_layer(place, sizes, down_parts, *up_blocks[0])
    up_parts = send_parts(*up_blocks, "g", "y")
    e2 = own_sum(grad_up, wu)

    d_gain_mlp = jnp.sum(e2 * normal_two, axis=0)
    d_shift_mlp = jnp.sum(e2, axis=0)
    grad_hidden = grad_own + norm_back(e2, normal_two, inverse_two, h_gain_mlp)
    grad_branch = half(depth * grad_hidden)
    d_bias_proj = jnp.sum(grad_branch, axis=0, dtype=F32)

    attended_back, d_proj = [], []
    for k in range(nt):
        at = lax.rem(t + k, nt) * part
        attended_back.append(half(dot(grad_branch, lax.dynamic_slice_in_dim(wo, at, part, 0), (1, 1))))
        d_proj.append(half(dot(attended, lax.dynamic_slice_in_dim(grad_branch, at, part, 1), (0, 0))))
    grad_attended = jnp.concatenate(
        [attended_back[0]] + [shift(b, "t", k) for k, b in enumerate(attended_back) if k], axis=0
    )
    d_proj = total_sum([d_proj[0].astype(F32)] + [shift(b, "t", k) for k, b in enumerate(d_proj) if k])

    def to_rows(blocks):
        return jnp.stack(by_place(return_relative([blocks[k] for k in range(ng)], "g"), "g", 1), axis=0)

    up_parts = reduce_in_layer(place, sizes, up_parts, grad_attended)
    down_parts = reduce_over_z(place, down_parts, grad_attended)
    grad_attended = after(grad_attended, up_parts[0][0], down_parts[0])
    d_qkv = attend_back(qkv, grad_attended, logs, first_token, order, local, head_dim)
    sum_down = total_sum(down_parts)
    a_blocks = weight_grad(place, sizes, normed_attn, d_qkv, half(d_proj))
    a_parts = send_parts(*a_blocks, "g", "y")
    up_parts = reduce_over_z(place, up_parts, *a_blocks[0])
    e1 = own_sum(d_qkv, wqkv)
    lowered = dot(after(active, e1), wd, (1, 0))
    lowered = total_sum(
        [lowered[:own]] + [shift(half(lowered[k * own : (k + 1) * own]), "t", -k) for k in range(1, nt)]
    )
    block_out = to_rows(half(hidden + depth * (lowered + h_bias_down)).reshape(ng, local, width))
    normal_one, inverse_one = norm_parts(x_own)
    d_gain_attn = jnp.sum(e1 * normal_one, axis=0)
    d_shift_attn = jnp.sum(e1, axis=0)
    grad_input = grad_hidden + norm_back(e1, normal_one, inverse_one, h_gain_attn)
    grad_input = to_rows(half(grad_input).reshape(ng, local, width)).astype(F32)
    a_parts = reduce_in_layer(place, sizes, a_parts, e1)
    sum_up = total_sum(up_parts)
    sum_a = total_sum(reduce_over_z(place, a_parts))

    def by_owner(full):
        return full.reshape(chips, nt, -1)

    d_bias_qkv = jnp.sum(d_qkv, axis=0, dtype=F32).reshape(pairs, 3, lanes)
    d_bias_qv = jnp.zeros((2 * width,), F32)
    d_bias_qv = lax.dynamic_update_slice_in_dim(d_bias_qv, d_bias_qkv[:, 0].reshape(-1), t * part, 0)
    d_bias_qv = lax.dynamic_update_slice_in_dim(d_bias_qv, d_bias_qkv[:, 2].reshape(-1), width + t * part, 0)
    d_bias_up = d_bias_up.reshape(chips, 1, ff_shard)
    d_bias_up = jnp.where(lax.broadcasted_iota(jnp.int32, (chips, nt, 1), 1) == t, d_bias_up, 0.0)
    d_bias_down = jnp.sum(grad_down[:own], axis=0, dtype=F32)
    sums = jnp.concatenate(
        [
            by_owner(d_gain_attn),
            by_owner(d_shift_attn),
            by_owner(d_bias_qv),
            by_owner(d_bias_proj),
            by_owner(d_gain_mlp),
            by_owner(d_shift_mlp),
            d_bias_up,
            by_owner(d_bias_down),
        ],
        axis=2,
    )
    sums = reduce_axis(sums, "t", 1).reshape(nz, ny, ng, count)
    for axis, at in (("g", 2), ("y", 1), ("z", 0)):
        sums = reduce_axis(sums, axis, at)
    out_vectors = [sums[offsets[i] : offsets[i + 1]] for i in range(len(counts))]

    up = swap_axis(sum_up.reshape(nt, shard, ff_part), "t", 0)
    sum_up = jnp.stack([u.reshape(shard, chips, ff_shard) for u in up], axis=2).reshape(shard, hidden_width)
    rest = swap_axis(sum_a.reshape(nt, shard, 4 * part), "t", 0)
    sum_qkv = jnp.stack([r[:, : 3 * part].reshape(shard, pairs, 3, lanes) for r in rest], axis=1)
    sum_qkv = sum_qkv.transpose(0, 3, 1, 2, 4).reshape(shard, 3 * width)
    sum_proj = jnp.concatenate([r[:, 3 * part :] for r in rest], axis=1)
    return (
        block_out,
        grad_input,
        out_vectors[0],
        out_vectors[1],
        sum_qkv,
        out_vectors[2],
        sum_proj,
        out_vectors[3],
        out_vectors[4],
        out_vectors[5],
        sum_up,
        out_vectors[6],
        sum_down,
        out_vectors[7],
    )


def solution(mesh):
    rows = 2
    dp, seq = mesh.shape["dp"], mesh.shape["seq"]
    high = 4
    split = Mesh(mesh.devices.reshape(high, dp // high, rows, seq // rows), ("z", "y", "g", "t"))
    everything = ("z", "y", "g", "t")
    tokens = P(("z", "y"), ("g", "t"), None)
    vector = P(everything)
    matrix = P(everything, None)
    return jax.shard_map(
        body,
        mesh=split,
        in_specs=(
            tokens,
            P(("z", "y"), None),
            vector,
            vector,
            matrix,
            vector,
            matrix,
            vector,
            vector,
            vector,
            matrix,
            vector,
            matrix,
            vector,
            tokens,
        ),
        out_specs=(
            tokens,
            tokens,
            vector,
            vector,
            matrix,
            vector,
            matrix,
            vector,
            vector,
            vector,
            matrix,
            vector,
            matrix,
            vector,
        ),
        check_vma=False,
    )
```

```python
import jax
import jax.numpy as jnp
from jax import lax
from jax.experimental import pallas as pl
from jax.experimental.pallas import tpu as pltpu
from jax.sharding import Mesh, PartitionSpec as P

H = 16
LAYERS = 24
EPSILON = 1e-05
DOC_MAX = 512

BF = jnp.bfloat16
F32 = jnp.float32


def half(values):
    return values.astype(BF)


def norm_parts(values):
    mean = jnp.mean(values, axis=-1, keepdims=True)
    centred = values - mean
    spread = jnp.mean(centred * centred, axis=-1, keepdims=True)
    inverse = lax.rsqrt(spread + EPSILON)
    return (centred * inverse, inverse)


def norm_back(grad_out, normal, inverse, gain):
    scaled = grad_out * gain
    return inverse * (
        scaled
        - jnp.mean(scaled, axis=-1, keepdims=True)
        - normal * jnp.mean(scaled * normal, axis=-1, keepdims=True)
    )


def dot(left, right, contract):
    return lax.dot_general(left, right, ((contract[:1], contract[1:]), ((), ())), preferred_element_type=F32)


def cost(microseconds):
    return pl.CostEstimate(flops=int(microseconds * 2.70e8), bytes_accessed=int(microseconds * 0.90e6), transcendentals=0)


def after(value, *others):
    return lax.optimization_barrier((value, *others))[0]


def shift(value, axis, step):
    size = lax.axis_size(axis)
    return lax.ppermute(value, axis, [(i, (i + step) % size) for i in range(size)])


def gather_relative(value, axis):
    return [value] + [shift(value, axis, k) for k in range(1, lax.axis_size(axis))]


def return_relative(blocks, axis):
    return [blocks[0]] + [shift(block, axis, -k) for k, block in enumerate(blocks) if k]


def by_place(parts, axis, sign):
    size = len(parts)
    here = lax.axis_index(axis)
    return [lax.select_n(lax.rem(sign * (place - here) + size, size), *parts) for place in range(size)]


def swap_axis(value, axis, at):
    size = lax.axis_size(axis)
    here = lax.axis_index(axis)
    parts = []
    for k in range(size):
        block = lax.dynamic_index_in_dim(value, lax.rem(here + k, size), at, keepdims=False)
        parts.append(shift(block, axis, k) if k else block)
    return by_place(parts, axis, -1)


def reduce_axis(value, axis, at):
    size = lax.axis_size(axis)
    here = lax.axis_index(axis)
    total = lax.dynamic_index_in_dim(value, here, at, keepdims=False)
    for k in range(1, size):
        block = lax.dynamic_index_in_dim(value, lax.rem(here + k, size), at, keepdims=False)
        total = total + shift(block, axis, k)
    return total


def whole(memory_space=pltpu.VMEM):
    return pl.BlockSpec(memory_space=memory_space)


def assemble(place, firsts, seconds, wanted, shapes):
    ny, ng = len(firsts), len(seconds)
    nz, high, wide = firsts[0].shape[1:]

    def kernel(place_ref, *refs):
        ins, outs = (refs[:ny], refs[ny : ny + ng]), refs[ny + ng :]
        y, g = place_ref[1], place_ref[2]
        for pieces, out in zip(wanted, outs):
            for which, row, rows, column, columns, into in pieces:
                for ky in range(ny):
                    for kg in range(ng):
                        source = ins[0][ky].at[kg, 0] if which == 0 else ins[1][kg].at[ky, 0]
                        at = (0, lax.rem(y - ky + ny, ny), lax.rem(g - kg + ng, ng))
                        out[(*at, slice(None), pl.ds(into, columns))] = source[row : row + rows, column : column + columns]

    def out_spec(shape):
        return pl.BlockSpec((1, ny, ng, *shape), lambda i, place_ref: (i, 0, 0, 0, 0))

    return pl.pallas_call(
        kernel,
        grid_spec=pltpu.PrefetchScalarGridSpec(
            num_scalar_prefetch=1,
            grid=(nz,),
            in_specs=[pl.BlockSpec((ng, 1, high, wide), lambda i, place_ref: (0, i, 0, 0))] * ny
            + [pl.BlockSpec((ny, 1, high, wide), lambda i, place_ref: (0, i, 0, 0))] * ng,
            out_specs=[out_spec(shape) for shape in shapes],
        ),
        out_shape=[jax.ShapeDtypeStruct((nz, ny, ng, *shape), BF) for shape in shapes],
        compiler_params=pltpu.CompilerParams(vmem_limit_bytes=16 << 20),
        cost_estimate=cost(4),
        name="assemble",
    )(place, *[*firsts, *seconds])


def gather_over_z(value):
    copies = jnp.broadcast_to(value[None], (lax.axis_size("z"), *value.shape))
    return lax.all_to_all(copies, "z", 0, 0, tiled=True)


def halves(values):
    middle = values.shape[-1] // 2
    return values[..., :middle], values[..., middle:]


def gather_once(first, second):
    return jnp.stack(gather_relative(first, "g")), jnp.stack(gather_relative(second, "y"))


def gather_twice(first, second):
    return gather_relative(first, "y"), gather_relative(second, "g")


def weight_grad_kernel(sizes, place_ref, left_ref, right_ref, *refs):
    nz, ny, ng = sizes
    middle = (len(refs) - 1) - (ny + ng)
    kept, outs, total = refs[:middle], refs[middle:-1], refs[-1]
    y, g = place_ref[1], place_ref[2]
    width = right_ref.shape[1]
    total[:, :width] = dot(left_ref[...], right_ref[...], (0, 0))
    if kept:
        total[:, width:] = kept[0][...].astype(F32)
    columns = total.shape[1] // 2
    rows = total.shape[0] // (ny * ng)
    for k in range(ng):
        at = lax.rem(g + k, ng)
        for i in range(ny):
            start = pl.multiple_of((i * ng + at) * rows, rows)
            outs[k][0, i] = half(total[pl.ds(start, rows), :columns])
    for k in range(ny):
        at = lax.rem(y + k, ny)
        for i in range(ng):
            start = pl.multiple_of((at * ng + i) * rows, rows)
            outs[ng + k][0, i] = half(total[pl.ds(start, rows), columns:])


def weight_grad(place, sizes, left, right, more=None):
    nz, ny, ng = sizes
    tokens, height = left.shape
    width = right.shape[1] + (more.shape[1] if more is not None else 0)
    rows, columns = height // (nz * ny * ng), width // 2

    def kernel(*refs):
        weight_grad_kernel(sizes, *refs)

    first = jax.ShapeDtypeStruct((nz, ny, rows, columns), BF)
    second = jax.ShapeDtypeStruct((nz, ng, rows, columns), BF)
    step = height // nz
    extra = [] if more is None else [more]
    outs = pl.pallas_call(
        kernel,
        grid=(nz,),
        in_specs=[
            whole(pltpu.SMEM),
            pl.BlockSpec((tokens, step), lambda i: (0, i)),
            pl.BlockSpec((tokens, right.shape[1]), lambda i: (0, 0)),
        ]
        + [pl.BlockSpec((step, m.shape[1]), lambda i: (i, 0)) for m in extra],
        out_specs=[pl.BlockSpec((1, ny, rows, columns), lambda i: (i, 0, 0, 0))] * ng
        + [pl.BlockSpec((1, ng, rows, columns), lambda i: (i, 0, 0, 0))] * ny,
        out_shape=[first] * ng + [second] * ny,
        scratch_shapes=[pltpu.VMEM((step, width), F32)],
        compiler_params=pltpu.CompilerParams(vmem_limit_bytes=20 << 20),
        cost_estimate=cost(7),
        name="weight_grad",
    )(place, *[left, right, *extra])
    return outs[:ng], outs[ng:]


def total_of(refs, at):
    value = refs[0][at].astype(F32)
    for ref in refs[1:]:
        value = value + ref[at].astype(F32)
    return value


def add_split(place, sizes, first, second):
    nz, ny, ng = sizes
    rows, columns = first[0].shape[2:]

    def kernel(place_ref, *refs):
        firsts, seconds, outs = refs[:ng], refs[ng : ng + ny], refs[ng + ny :]
        y, g = place_ref[1], place_ref[2]
        for k in range(ny):
            outs[k][0] = half(total_of(firsts, (0, lax.rem(y + k, ny))))
        for k in range(ng):
            outs[ny + k][0] = half(total_of(seconds, (0, lax.rem(g + k, ng))))

    shape = jax.ShapeDtypeStruct((nz, rows, columns), BF)
    outs = pl.pallas_call(
        kernel,
        grid=(nz,),
        in_specs=[whole(pltpu.SMEM)]
        + [pl.BlockSpec((1, ny, rows, columns), lambda i: (i, 0, 0, 0))] * ng
        + [pl.BlockSpec((1, ng, rows, columns), lambda i: (i, 0, 0, 0))] * ny,
        out_specs=[pl.BlockSpec((1, rows, columns), lambda i: (i, 0, 0))] * (ny + ng),
        out_shape=[shape] * (ny + ng),
        compiler_params=pltpu.CompilerParams(vmem_limit_bytes=12 << 20),
        cost_estimate=cost(3.5),
        name="add_split",
    )(place, *[*first, *second])
    return outs[:ny], outs[ny:]


def split_over_z(first, second, more):
    ny, ng = len(first), len(second)
    nz, rows, columns = first[0].shape
    extra = [] if more is None else [more]
    count = 0 if more is None else more.shape[1]
    n_in = ny + ng + len(extra)

    def kernel(*refs):
        out = refs[n_in]
        out[0, :rows, :columns] = half(total_of(refs[:ny], 0))
        out[0, :rows, columns:] = half(total_of(refs[ny : ny + ng], 0))
        if extra:
            out[0, rows:] = half(refs[n_in - 1][0])

    return pl.pallas_call(
        kernel,
        grid=(nz,),
        in_specs=[pl.BlockSpec((1, rows, columns), lambda i: (i, 0, 0))] * (ny + ng)
        + [pl.BlockSpec((1, *m.shape[1:]), lambda i: (i, 0, 0)) for m in extra],
        out_specs=pl.BlockSpec((1, rows + count, 2 * columns), lambda i: (i, 0, 0)),
        out_shape=jax.ShapeDtypeStruct((nz, rows + count, 2 * columns), BF),
        compiler_params=pltpu.CompilerParams(vmem_limit_bytes=12 << 20),
        cost_estimate=cost(2.5),
        name="split_over_z",
    )(*first, *second, *extra)


def send_parts(first, second, axis_first, axis_second):
    first = [first[0]] + [shift(b, axis_first, k) for k, b in enumerate(first) if k]
    second = [second[0]] + [shift(b, axis_second, k) for k, b in enumerate(second) if k]
    return first, second


def reduce_in_layer(place, sizes, parts, *others):
    first, second = parts
    first = [after(first[0], *others)] + first[1:]
    return send_parts(*add_split(place, sizes, first, second), "y", "g")


def sum_over_z(blocks):
    return jnp.sum(lax.all_to_all(blocks, "z", 0, 0, tiled=True).astype(F32), axis=0)


def total_sum(blocks):
    total = blocks[0]
    for block in blocks[1:]:
        total = total + block.astype(F32)
    return total


def key_blocks(start, block):
    return range(max(0, start - DOC_MAX), start + block, block)


def visible_part(first_ref, low, start, block, rows, row):
    key_pos = low + row + lax.broadcasted_iota(jnp.int32, (rows, block), 0)
    visible = key_pos >= first_ref[:, start : start + block]
    if low == start:
        visible &= key_pos <= start + lax.broadcasted_iota(jnp.int32, (rows, block), 1)
    return visible


def fold(values, op):
    rows, lanes = values.shape
    return op(values.reshape(rows // 8, 8, lanes), axis=0)


def for_heads(values, head_dim):
    lane = lax.broadcasted_iota(jnp.int32, values.shape, 1) // head_dim
    heads = values.shape[1] // head_dim
    return jnp.concatenate([jnp.where(lane == h, values, jnp.zeros_like(values)) for h in range(heads)], axis=0)


def heads_of(values, head_dim, block):
    heads = values.shape[0] // head_dim
    return jnp.concatenate(
        [values[h * head_dim : (h + 1) * head_dim, h * block : (h + 1) * block] for h in range(heads)], axis=0
    )


def load_in_order(order_ref, source, into, local, columns):
    for n in range(into.shape[0] // local):
        rows = pl.ds(pl.multiple_of(order_ref[n] * local, local), local)
        into[n * local : (n + 1) * local] = source[rows, columns]


def store_in_order(order_ref, source, into, local, columns):
    for n in range(source.shape[0] // local):
        rows = pl.ds(pl.multiple_of(order_ref[n] * local, local), local)
        into[rows, columns] = half(source[n * local : (n + 1) * local])


def attend_kernel(block, sub, head_dim, local, order_ref, qkv_ref, first_ref, out_ref, log_ref, q_s, k_s, v_s, o_s, s_s):
    length, lanes = q_s.shape
    heads = lanes // head_dim
    for i, into in enumerate((q_s, k_s, v_s)):
        load_in_order(order_ref, qkv_ref, into, local, slice(i * lanes, (i + 1) * lanes))
    v_t = v_s[...].T
    for start in range(0, length, block):
        q_heads = for_heads(q_s[start : start + block] * (head_dim ** (-0.5)), head_dim)
        lows = list(key_blocks(start, block))
        top8 = [jnp.full((8, block), -1e30, F32)] * heads
        for n, low in enumerate(lows):
            scores = dot(k_s[low : low + block], q_heads, (1, 1))
            for r in range(0, block, sub):
                visible = visible_part(first_ref, low, start, block, sub, r)
                rows = slice(n * block + r, n * block + r + sub)
                for h in range(heads):
                    columns = slice(h * block, (h + 1) * block)
                    piece = jnp.where(visible, scores[r : r + sub, columns], -1e30)
                    top8[h] = jnp.maximum(top8[h], fold(piece, jnp.max))
                    s_s[rows, columns] = piece
        width = len(lows) * block
        top = jnp.concatenate([jnp.max(v, axis=0, keepdims=True) for v in top8], axis=1)
        total8 = jnp.zeros((8, heads * block), F32)
        for r in range(0, width, sub):
            exponent = jnp.exp(s_s[r : r + sub] - top)
            total8 = total8 + fold(exponent, jnp.sum)
            s_s[r : r + sub] = exponent
        total = jnp.sum(total8, axis=0, keepdims=True)
        probs = half(s_s[:width] * (1.0 / total))
        out = dot(v_t[:, lows[0] : lows[0] + width], probs, (1, 0))
        log = top + jnp.log(total)
        for h in range(heads):
            log_ref[0, h : h + 1, start : start + block] = log[:, h * block : (h + 1) * block]
        o_s[start : start + block] = half(heads_of(out, head_dim, block).T)
    store_in_order(order_ref, o_s, out_ref, local, slice(None))


def attend_back_kernel(
    block,
    sub,
    head_dim,
    local,
    order_ref,
    qkv_ref,
    g_ref,
    log_ref,
    first_ref,
    out_ref,
    q_s,
    k_s,
    v_s,
    g_s,
    query_grad,
    key_sum,
    value_sum,
    p_s,
    d_s,
):
    length, lanes = q_s.shape
    heads = lanes // head_dim
    scale = head_dim ** (-0.5)
    for i, into in enumerate((q_s, k_s, v_s)):
        load_in_order(order_ref, qkv_ref, into, local, slice(i * lanes, (i + 1) * lanes))
    load_in_order(order_ref, g_ref, g_s, local, slice(None))
    k_t = k_s[...].T
    for start in range(0, length, block):
        q_heads = for_heads(q_s[start : start + block] * scale, head_dim)
        g_heads = for_heads(g_s[start : start + block], head_dim)
        lows = list(key_blocks(start, block))
        delta8 = [jnp.zeros((8, block), F32)] * heads
        for n, low in enumerate(lows):
            scores = dot(k_s[low : low + block], q_heads, (1, 1))
            grads = dot(v_s[low : low + block], g_heads, (1, 1))
            for r in range(0, block, sub):
                visible = visible_part(first_ref, low, start, block, sub, r)
                rows = slice(n * block + r, n * block + r + sub)
                for h in range(heads):
                    columns = slice(h * block, (h + 1) * block)
                    p = jnp.where(visible, scores[r : r + sub, columns], -1e30)
                    p = jnp.exp(p - log_ref[0, h : h + 1, start : start + block])
                    d = grads[r : r + sub, columns]
                    delta8[h] = delta8[h] + fold(p * d, jnp.sum)
                    p_s[rows, columns] = p
                    d_s[rows, columns] = d
        delta = jnp.concatenate([jnp.sum(v, axis=0, keepdims=True) for v in delta8], axis=1)
        width = len(lows) * block
        p = p_s[:width]
        grad_scores = half(p * (d_s[:width] - delta))
        dq = dot(k_t[:, lows[0] : lows[0] + width], grad_scores, (1, 0))
        dk = dot(grad_scores, q_heads, (1, 0))
        dv = dot(half(p), g_heads, (1, 0))
        for n, low in enumerate(lows):
            rows = slice(n * block, (n + 1) * block)
            if low == start:
                key_sum[low : low + block] = dk[rows]
                value_sum[low : low + block] = dv[rows]
            else:
                key_sum[low : low + block] += dk[rows]
                value_sum[low : low + block] += dv[rows]
        query_grad[start : start + block] = (heads_of(dq, head_dim, block) * scale).T
    for i, source in enumerate((query_grad, key_sum, value_sum)):
        store_in_order(order_ref, source, out_ref, local, slice(i * lanes, (i + 1) * lanes))


def attend(qkv, first, order, local, head_dim):
    length, width = qkv.shape
    block = min(256, length)
    window = min(length, DOC_MAX + block)
    lanes = 2 * head_dim
    steps = width // (3 * lanes)

    def kernel(*refs):
        attend_kernel(block, 64, head_dim, local, *refs)

    return pl.pallas_call(
        kernel,
        grid=(steps,),
        in_specs=[
            whole(pltpu.SMEM),
            pl.BlockSpec((length, 3 * lanes), lambda i: (0, i)),
            pl.BlockSpec((1, length), lambda i: (0, 0)),
        ],
        out_specs=[
            pl.BlockSpec((length, lanes), lambda i: (0, i)),
            pl.BlockSpec((1, 2, length), lambda i: (i, 0, 0)),
        ],
        out_shape=[
            jax.ShapeDtypeStruct((length, width // 3), BF),
            jax.ShapeDtypeStruct((steps, 2, length), F32),
        ],
        scratch_shapes=[pltpu.VMEM((length, lanes), BF)] * 4 + [pltpu.VMEM((window, 2 * block), F32)],
        compiler_params=pltpu.CompilerParams(vmem_limit_bytes=16 << 20),
        cost_estimate=cost(11.5 * steps / 4),
        name="attend",
    )(order, qkv, first[None])


def attend_back(qkv, grad_out, logs, first, order, local, head_dim):
    length, width = qkv.shape
    block = min(256, length)
    window = min(length, DOC_MAX + block)
    lanes = 2 * head_dim
    steps = width // (3 * lanes)

    def kernel(*refs):
        attend_back_kernel(block, 64, head_dim, local, *refs)

    return pl.pallas_call(
        kernel,
        grid=(steps,),
        in_specs=[
            whole(pltpu.SMEM),
            pl.BlockSpec((length, 3 * lanes), lambda i: (0, i)),
            pl.BlockSpec((length, lanes), lambda i: (0, i)),
            pl.BlockSpec((1, 2, length), lambda i: (i, 0, 0)),
            pl.BlockSpec((1, length), lambda i: (0, 0)),
        ],
        out_specs=pl.BlockSpec((length, 3 * lanes), lambda i: (0, i)),
        out_shape=jax.ShapeDtypeStruct((length, width), BF),
        scratch_shapes=[pltpu.VMEM((length, lanes), BF)] * 4
        + [pltpu.VMEM((length, lanes), F32)] * 3
        + [pltpu.VMEM((window, 2 * block), F32)] * 2,
        compiler_params=pltpu.CompilerParams(vmem_limit_bytes=20 << 20),
        cost_estimate=cost(18 * steps / 4),
        name="attend_back",
    )(order, qkv, grad_out, logs, first[None])


def gelu_parts(u):
    c = 0.7978845608028654
    square = u * u
    h = 0.5 + 0.5 * jnp.tanh(u * (c + (c * 0.044715) * square))
    value = u * h
    return value, h + value * (1.0 - h) * (2 * c + (6 * c * 0.044715) * square)


def up_part(normed, weight, bias):
    tokens, width = normed.shape
    ff = weight.shape[1]
    block = min(256, ff)
    rows = min(256, tokens)

    def kernel(x_ref, w_ref, b_ref, active_ref, slope_ref):
        for r in range(0, tokens, rows):
            u = dot(x_ref[r : r + rows], w_ref[...], (1, 0)) + b_ref[...]
            value, slope = gelu_parts(u)
            active_ref[r : r + rows] = half(value)
            slope_ref[r : r + rows] = slope

    column = pl.BlockSpec((tokens, block), lambda i: (0, i))
    return pl.pallas_call(
        kernel,
        grid=(ff // block,),
        in_specs=[
            pl.BlockSpec((tokens, width), lambda i: (0, 0)),
            pl.BlockSpec((width, block), lambda i: (0, i)),
            pl.BlockSpec((1, block), lambda i: (0, i)),
        ],
        out_specs=[column, column],
        out_shape=[jax.ShapeDtypeStruct((tokens, ff), BF), jax.ShapeDtypeStruct((tokens, ff), F32)],
        compiler_params=pltpu.CompilerParams(vmem_limit_bytes=16 << 20),
        cost_estimate=cost(7),
        name="up_part",
    )(*[normed, weight], bias[None])


def up_back(grad_down, weight, slope):
    tokens, width = grad_down.shape
    ff = weight.shape[0]
    block = min(256, ff)
    rows = min(256, tokens)

    def kernel(g_ref, w_ref, slope_ref, out_ref, sum_ref):
        total = jnp.zeros((8, block), F32)
        for r in range(0, tokens, rows):
            grad = half(dot(g_ref[r : r + rows], w_ref[...], (1, 1)) * slope_ref[r : r + rows])
            out_ref[r : r + rows] = grad
            total = total + fold(grad.astype(F32), jnp.sum)
        sum_ref[...] = jnp.sum(total, axis=0, keepdims=True)

    column = pl.BlockSpec((tokens, block), lambda i: (0, i))
    return pl.pallas_call(
        kernel,
        grid=(ff // block,),
        in_specs=[
            pl.BlockSpec((tokens, width), lambda i: (0, 0)),
            pl.BlockSpec((block, width), lambda i: (i, 0)),
            column,
        ],
        out_specs=[column, pl.BlockSpec((1, block), lambda i: (0, i))],
        out_shape=[jax.ShapeDtypeStruct((tokens, ff), BF), jax.ShapeDtypeStruct((1, ff), F32)],
        compiler_params=pltpu.CompilerParams(vmem_limit_bytes=16 << 20),
        cost_estimate=cost(6.5),
        name="up_back",
    )(*[grad_down, weight, slope])


def body(
    block_input,
    doc_ids,
    gain_attn,
    shift_attn,
    w_qkv,
    bias_qv,
    w_proj,
    bias_proj,
    gain_mlp,
    shift_mlp,
    w_up,
    bias_up,
    w_down,
    bias_down,
    out_grad,
):
    nz, ny, ng, nt = (lax.axis_size(a) for a in ("z", "y", "g", "t"))
    sizes = (nz, ny, ng)
    z, y, g, t = (lax.axis_index(a) for a in ("z", "y", "g", "t"))
    place = jnp.stack([z, y, g]).astype(jnp.int32)
    chips = nz * ny * ng
    depth = LAYERS ** (-0.5)
    _, local, width = block_input.shape
    length = doc_ids.shape[1]
    shard = w_qkv.shape[0]
    part = width // nt
    head_dim = width // H
    lanes = 2 * head_dim
    pairs = part // lanes
    hidden_width = w_up.shape[1]
    ff_shard = w_down.shape[0]
    ff_part = hidden_width // nt
    own = ng * local
    block_rows = nt * shard

    natural = jnp.arange(ng * nt, dtype=jnp.int32)
    order = lax.rem(t - natural % nt + nt, nt) * ng + lax.rem(g - natural // nt + ng, ng)
    docs = lax.dynamic_index_in_dim(doc_ids, g, 0, keepdims=False)
    first_token = jnp.sum((docs[None, :] < docs[:, None]).astype(jnp.int32), axis=1)

    both = jnp.stack([block_input, out_grad], axis=1)
    parts = []
    for k in range(ng):
        block = lax.dynamic_index_in_dim(both, lax.rem(g + k, ng), 0, keepdims=False)
        parts.append(shift(block, "g", k) if k else block)
    both_own = jnp.concatenate(parts, axis=1)
    x_own, grad_own = both_own[0].astype(F32), both_own[1].astype(F32)
    both_all = jnp.concatenate(gather_relative(both_own, "t"), axis=1)

    vectors = [gain_attn, shift_attn, bias_qv, bias_proj, gain_mlp, shift_mlp, bias_up, bias_down]
    counts = [v.shape[0] for v in vectors]
    packed = half(lax.optimization_barrier(jnp.concatenate(vectors)))
    count = packed.shape[0]
    columns_a = half(w_qkv).reshape(shard, 3, nt, pairs, lanes).transpose(2, 0, 3, 1, 4).reshape(nt, shard, 3 * part)
    columns_o = half(w_proj).reshape(shard, nt, part).transpose(1, 0, 2)
    columns_u = half(w_up).reshape(shard, chips, nt, ff_shard).transpose(2, 0, 1, 3).reshape(nt, shard, ff_part)
    columns = jnp.concatenate([columns_a, columns_o, columns_u], axis=2)
    wide = columns.shape[2]
    packed = jnp.broadcast_to(jnp.pad(packed, (0, wide - count)), (nt, 8, wide))
    columns = swap_axis(jnp.concatenate([columns, packed], axis=1), "t", 0)
    packed = jnp.concatenate([c[shard : shard + 1, :count] for c in columns], axis=1)
    columns = jnp.concatenate([c[:shard] for c in columns], axis=0)
    packed = jnp.broadcast_to(jnp.pad(packed, ((0, 0), (0, 4 * part - nt * count))), (8, 4 * part))
    shard_a = jnp.concatenate([columns[:, : 4 * part], packed], axis=0)
    shard_u = columns[:, 4 * part :]
    shard_d = half(w_down)
    middle_d = width // 2

    first_d, second_d = gather_once(shard_d[:, :middle_d], shard_d[:, middle_d:])
    first_a, second_a = halves(gather_over_z(after(shard_a, first_d, second_d)))
    first_u, second_u = halves(gather_over_z(after(shard_u, first_a, second_a)))
    first_a, second_a = gather_once(first_a, second_a)
    both_d = jnp.concatenate([first_d, second_d], axis=0)
    both_d = gather_over_z(after(both_d, first_u, second_u, first_a, second_a))
    first_a, second_a = gather_twice(first_a, second_a)
    side = 3 * part - 2 * part
    wqkv, wo, vector_rows = assemble(
        place,
        first_a,
        second_a,
        [
            [(0, 0, block_rows, 0, 2 * part, 0), (1, 0, block_rows, 0, side, 2 * part)],
            [(1, 0, block_rows, side, part, 0)],
            [(0, block_rows, 8, 0, 2 * part, 0)],
        ],
        [(block_rows, 3 * part), (block_rows, part), (8, 2 * part)],
    )
    wqkv = wqkv.reshape(width, 3 * part)
    wo = wo.reshape(width, part)
    first_u, second_u = gather_once(after(first_u, *first_a, *second_a), after(second_u, *first_a, *second_a))

    vector_rows = vector_rows.reshape(chips, 8, 2 * part)[:, 0, : nt * count].reshape(chips, nt, count)
    offsets = [0]
    for size in counts:
        offsets.append(offsets[-1] + size)
    pieces = [vector_rows[:, :, offsets[i] : offsets[i + 1]] for i in range(len(counts))]
    h_gain_attn, h_shift_attn, h_bias_qv, h_bias_proj, h_gain_mlp, h_shift_mlp = (
        p.reshape(-1).astype(F32) for p in pieces[:6]
    )
    h_bias_down = pieces[7].reshape(-1).astype(F32)
    h_bias_up = lax.dynamic_index_in_dim(pieces[6], t, 1, keepdims=False).astype(F32).reshape(-1)
    bias_q = lax.dynamic_slice_in_dim(h_bias_qv, t * part, part).reshape(pairs, lanes)
    bias_v = lax.dynamic_slice_in_dim(h_bias_qv, width + t * part, part).reshape(pairs, lanes)
    bias_qkv = jnp.stack([bias_q, jnp.zeros_like(bias_q), bias_v], axis=1).reshape(-1)

    normal_all, _ = norm_parts(both_all[0].astype(F32))
    normed_attn = half(normal_all * h_gain_attn + h_shift_attn)
    grad_down = half(depth * both_all[1].astype(F32))
    qkv = half(dot(after(normed_attn, first_u, second_u), wqkv, (1, 0)) + bias_qkv)
    attended_heads, logs = attend(qkv, first_token, order, local, head_dim)
    first_u, second_u = gather_twice(first_u, second_u)
    wo = jnp.concatenate(by_place(gather_relative(wo, "t"), "t", -1), axis=1)
    attended = return_relative([attended_heads[k * own : (k + 1) * own] for k in range(nt)], "t")
    attended = jnp.concatenate(by_place(attended, "t", 1), axis=1)
    hidden = x_own + depth * (dot(attended, wo, (1, 0)) + h_bias_proj)
    normal_two, inverse_two = norm_parts(hidden)
    normed_own = half(normal_two * h_gain_mlp + h_shift_mlp)
    normed_mlp = jnp.concatenate(gather_relative(normed_own, "t"), axis=0)
    (wu,) = assemble(
        place,
        first_u,
        second_u,
        [[(0, 0, block_rows, 0, ff_part // 2, 0), (1, 0, block_rows, 0, ff_part // 2, ff_part // 2)]],
        [(block_rows, ff_part)],
    )
    wu = wu.reshape(width, ff_part)
    first_d, second_d = both_d[:, :ng].swapaxes(0, 1), both_d[:, ng:].swapaxes(0, 1)
    first_d, second_d = gather_twice(after(first_d, *first_u, *second_u), after(second_d, *first_u, *second_u))
    active, slope = up_part(normed_mlp, wu, h_bias_up)

    def own_sum(left, right):
        blocks = [half(dot(left[k * own : (k + 1) * own], right, (1, 1))) for k in range(1, nt)]
        mine = dot(after(left[:own], *blocks), right, (1, 1))
        return total_sum([mine] + [shift(block, "t", -k - 1) for k, block in enumerate(blocks)])

    down_blocks = weight_grad(place, sizes, active, grad_down)
    down_parts = send_parts(*down_blocks, "g", "y")
    (wd,) = assemble(
        place,
        first_d,
        second_d,
        [[(0, 0, ff_shard, 0, middle_d, 0), (1, 0, ff_shard, 0, middle_d, middle_d)]],
        [(ff_shard, width)],
    )
    wd = wd.reshape(ff_part, width)
    grad_up, d_bias_up = up_back(after(grad_down, *down_blocks[0]), wd, slope)
    up_blocks = weight_grad(place, sizes, normed_mlp, grad_up)
    down_parts = reduce_in_layer(place, sizes, down_parts, *up_blocks[0])
    up_parts = send_parts(*up_blocks, "g", "y")
    e2 = own_sum(grad_up, wu)

    d_gain_mlp = jnp.sum(e2 * normal_two, axis=0)
    d_shift_mlp = jnp.sum(e2, axis=0)
    grad_hidden = grad_own + norm_back(e2, normal_two, inverse_two, h_gain_mlp)
    grad_branch = half(depth * grad_hidden)
    d_bias_proj = jnp.sum(grad_branch, axis=0, dtype=F32)

    attended_back, d_proj = [], []
    for k in range(nt):
        at = lax.rem(t + k, nt) * part
        attended_back.append(half(dot(grad_branch, lax.dynamic_slice_in_dim(wo, at, part, 0), (1, 1))))
        d_proj.append(half(dot(attended, lax.dynamic_slice_in_dim(grad_branch, at, part, 1), (0, 0))))
    grad_attended = jnp.concatenate(
        [attended_back[0]] + [shift(b, "t", k) for k, b in enumerate(attended_back) if k], axis=0
    )
    d_proj = total_sum([d_proj[0].astype(F32)] + [shift(b, "t", k) for k, b in enumerate(d_proj) if k])

    def to_rows(blocks):
        return jnp.stack(by_place(return_relative([blocks[k] for k in range(ng)], "g"), "g", 1), axis=0)

    up_parts = reduce_in_layer(place, sizes, up_parts, grad_attended)
    down_blocks = split_over_z(*down_parts, None)
    sum_down = sum_over_z(down_blocks)
    grad_attended = after(grad_attended, up_parts[0][0], down_blocks)
    d_qkv = attend_back(qkv, grad_attended, logs, first_token, order, local, head_dim)
    a_blocks = weight_grad(place, sizes, normed_attn, d_qkv, half(d_proj))
    a_parts = send_parts(*a_blocks, "g", "y")
    up_blocks = split_over_z([after(up_parts[0][0], *a_blocks[0])] + up_parts[0][1:], up_parts[1], None)
    sum_up = sum_over_z(up_blocks)
    e1 = own_sum(after(d_qkv, up_blocks), wqkv)
    normal_one, inverse_one = norm_parts(x_own)
    d_gain_attn = jnp.sum(e1 * normal_one, axis=0)
    d_shift_attn = jnp.sum(e1, axis=0)
    grad_input = grad_hidden + norm_back(e1, normal_one, inverse_one, h_gain_attn)
    a_parts = reduce_in_layer(place, sizes, a_parts, e1)
    lowered = dot(after(active, a_parts[0][0]), wd, (1, 0))
    lowered = total_sum(
        [lowered[:own]] + [shift(half(lowered[k * own : (k + 1) * own]), "t", -k) for k in range(1, nt)]
    )
    block_out = to_rows(half(hidden + depth * (lowered + h_bias_down)).reshape(ng, local, width))
    grad_input = to_rows(half(grad_input).reshape(ng, local, width)).astype(F32)

    def by_owner(full):
        return full.reshape(chips, nt, -1)

    d_bias_qkv = jnp.sum(d_qkv, axis=0, dtype=F32).reshape(pairs, 3, lanes)
    d_bias_qv = jnp.zeros((2 * width,), F32)
    d_bias_qv = lax.dynamic_update_slice_in_dim(d_bias_qv, d_bias_qkv[:, 0].reshape(-1), t * part, 0)
    d_bias_qv = lax.dynamic_update_slice_in_dim(d_bias_qv, d_bias_qkv[:, 2].reshape(-1), width + t * part, 0)
    d_bias_up = d_bias_up.reshape(chips, 1, ff_shard)
    d_bias_up = jnp.where(lax.broadcasted_iota(jnp.int32, (chips, nt, 1), 1) == t, d_bias_up, 0.0)
    d_bias_down = jnp.sum(grad_down[:own], axis=0, dtype=F32)
    sums = jnp.concatenate(
        [
            by_owner(d_gain_attn),
            by_owner(d_shift_attn),
            by_owner(d_bias_qv),
            by_owner(d_bias_proj),
            by_owner(d_gain_mlp),
            by_owner(d_shift_mlp),
            d_bias_up,
            by_owner(d_bias_down),
        ],
        axis=2,
    )
    sums = reduce_axis(sums, "t", 1).reshape(nz, ny, ng, count)
    sums = reduce_axis(reduce_axis(sums, "g", 2), "y", 1)
    high = half(sums)
    more = jnp.stack([high.astype(F32), sums - high.astype(F32)], axis=1)
    more = jnp.pad(more, ((0, 0), (0, 6), (0, 4 * part - count)))
    sum_a = sum_over_z(split_over_z(*a_parts, more))
    sums = sum_a[block_rows, :count] + sum_a[block_rows + 1, :count]
    sum_a = sum_a[:block_rows]
    out_vectors = [sums[offsets[i] : offsets[i + 1]] for i in range(len(counts))]

    up = swap_axis(sum_up.reshape(nt, shard, ff_part), "t", 0)
    sum_up = jnp.stack([u.reshape(shard, chips, ff_shard) for u in up], axis=2).reshape(shard, hidden_width)
    rest = swap_axis(sum_a.reshape(nt, shard, 4 * part), "t", 0)
    sum_qkv = jnp.stack([r[:, : 3 * part].reshape(shard, pairs, 3, lanes) for r in rest], axis=1)
    sum_qkv = sum_qkv.transpose(0, 3, 1, 2, 4).reshape(shard, 3 * width)
    sum_proj = jnp.concatenate([r[:, 3 * part :] for r in rest], axis=1)
    return (
        block_out,
        grad_input,
        out_vectors[0],
        out_vectors[1],
        sum_qkv,
        out_vectors[2],
        sum_proj,
        out_vectors[3],
        out_vectors[4],
        out_vectors[5],
        sum_up,
        out_vectors[6],
        sum_down,
        out_vectors[7],
    )


def solution(mesh):
    rows = 2
    dp, seq = mesh.shape["dp"], mesh.shape["seq"]
    high = 4
    split = Mesh(mesh.devices.reshape(high, dp // high, rows, seq // rows), ("z", "y", "g", "t"))
    everything = ("z", "y", "g", "t")
    tokens = P(("z", "y"), ("g", "t"), None)
    vector = P(everything)
    matrix = P(everything, None)
    return jax.shard_map(
        body,
        mesh=split,
        in_specs=(
            tokens,
            P(("z", "y"), None),
            vector,
            vector,
            matrix,
            vector,
            matrix,
            vector,
            vector,
            vector,
            matrix,
            vector,
            matrix,
            vector,
            tokens,
        ),
        out_specs=(
            tokens,
            tokens,
            vector,
            vector,
            matrix,
            vector,
            matrix,
            vector,
            vector,
            vector,
            matrix,
            vector,
            matrix,
            vector,
        ),
        check_vma=False,
    )
```

```python
import jax
import jax.numpy as jnp
from jax import lax
from jax.experimental import pallas as pl
from jax.experimental.pallas import tpu as pltpu
from jax.sharding import Mesh, PartitionSpec as P

H = 16
LAYERS = 24
EPSILON = 1e-05
DOC_MAX = 512

BF = jnp.bfloat16
F32 = jnp.float32


def half(values):
    return values.astype(BF)


def norm_parts(values):
    mean = jnp.mean(values, axis=-1, keepdims=True)
    centred = values - mean
    spread = jnp.mean(centred * centred, axis=-1, keepdims=True)
    inverse = lax.rsqrt(spread + EPSILON)
    return (centred * inverse, inverse)


def norm_back(grad_out, normal, inverse, gain):
    scaled = grad_out * gain
    return inverse * (
        scaled
        - jnp.mean(scaled, axis=-1, keepdims=True)
        - normal * jnp.mean(scaled * normal, axis=-1, keepdims=True)
    )


def dot(left, right, contract):
    return lax.dot_general(left, right, ((contract[:1], contract[1:]), ((), ())), preferred_element_type=F32)


def cost(microseconds):
    return pl.CostEstimate(flops=int(microseconds * 0.9e8), bytes_accessed=int(microseconds * 0.3e6), transcendentals=0)


def after(value, *others):
    return lax.optimization_barrier((value, *others))[0]


def shift(value, axis, step):
    size = lax.axis_size(axis)
    return lax.ppermute(value, axis, [(i, (i + step) % size) for i in range(size)])


def gather_relative(value, axis):
    return [value] + [shift(value, axis, k) for k in range(1, lax.axis_size(axis))]


def return_relative(blocks, axis):
    return [blocks[0]] + [shift(block, axis, -k) for k, block in enumerate(blocks) if k]


def by_place(parts, axis, sign):
    size = len(parts)
    here = lax.axis_index(axis)
    return [lax.select_n(lax.rem(sign * (place - here) + size, size), *parts) for place in range(size)]


def swap_axis(value, axis, at):
    size = lax.axis_size(axis)
    here = lax.axis_index(axis)
    parts = []
    for k in range(size):
        block = lax.dynamic_index_in_dim(value, lax.rem(here + k, size), at, keepdims=False)
        parts.append(shift(block, axis, k) if k else block)
    return by_place(parts, axis, -1)


def reduce_axes(value, axes, at):
    size = 1
    for axis in axes:
        size = size * lax.axis_size(axis)
    here = lax.axis_index(axes)
    total = lax.dynamic_index_in_dim(value, here, at, keepdims=False)
    for k in range(1, size):
        block = lax.dynamic_index_in_dim(value, lax.rem(here + k, size), at, keepdims=False)
        total = total + lax.ppermute(block, axes, [(i, (i + k) % size) for i in range(size)])
    return total


def reduce_axis(value, axis, at):
    size = lax.axis_size(axis)
    here = lax.axis_index(axis)
    total = lax.dynamic_index_in_dim(value, here, at, keepdims=False)
    for k in range(1, size):
        block = lax.dynamic_index_in_dim(value, lax.rem(here + k, size), at, keepdims=False)
        total = total + shift(block, axis, k)
    return total


def whole(memory_space=pltpu.VMEM):
    return pl.BlockSpec(memory_space=memory_space)


def assemble(place, firsts, seconds, wanted, shapes):
    ny, ng = len(firsts), len(seconds)
    nz, high, wide = firsts[0].shape[1:]

    def kernel(place_ref, *refs):
        ins, outs = (refs[:ny], refs[ny : ny + ng]), refs[ny + ng :]
        y, g = place_ref[1], place_ref[2]
        for pieces, out in zip(wanted, outs):
            for which, row, rows, column, columns, into in pieces:
                for ky in range(ny):
                    for kg in range(ng):
                        source = ins[0][ky].at[kg, 0] if which == 0 else ins[1][kg].at[ky, 0]
                        at = (0, lax.rem(y - ky + ny, ny), lax.rem(g - kg + ng, ng))
                        out[(*at, slice(None), pl.ds(into, columns))] = source[row : row + rows, column : column + columns]

    def out_spec(shape):
        return pl.BlockSpec((1, ny, ng, *shape), lambda i, place_ref: (i, 0, 0, 0, 0))

    return pl.pallas_call(
        kernel,
        grid_spec=pltpu.PrefetchScalarGridSpec(
            num_scalar_prefetch=1,
            grid=(nz,),
            in_specs=[pl.BlockSpec((ng, 1, high, wide), lambda i, place_ref: (0, i, 0, 0))] * ny
            + [pl.BlockSpec((ny, 1, high, wide), lambda i, place_ref: (0, i, 0, 0))] * ng,
            out_specs=[out_spec(shape) for shape in shapes],
        ),
        out_shape=[jax.ShapeDtypeStruct((nz, ny, ng, *shape), BF) for shape in shapes],
        compiler_params=pltpu.CompilerParams(vmem_limit_bytes=16 << 20),
        cost_estimate=cost(4),
        name="assemble",
    )(place, *[*firsts, *seconds])


def gather_over_z(value):
    copies = jnp.broadcast_to(value[None], (lax.axis_size("z"), *value.shape))
    return lax.all_to_all(copies, "z", 0, 0, tiled=True)


def halves(values):
    middle = values.shape[-1] // 2
    return values[..., :middle], values[..., middle:]


def gather_once(first, second):
    return jnp.stack(gather_relative(first, "g")), jnp.stack(gather_relative(second, "y"))


def gather_twice(first, second):
    return gather_relative(first, "y"), gather_relative(second, "g")


def weight_grad(place, sizes, left, right, more=()):
    nz, ny, ng = sizes
    n, m = len(left), len(more)
    tokens, height = left[0].shape
    right_width = right.shape[1]
    width = right_width + (more[0].shape[1] if more else 0)
    rows, columns = height // (nz * ny * ng), width // 2

    def kernel(place_ref, *refs):
        lefts, right_ref, mores, outs, total = refs[:n], refs[n], refs[n + 1 : n + 1 + m], refs[n + 1 + m : -1], refs[-1]
        y, g = place_ref[1], place_ref[2]
        value = dot(lefts[0][...], right_ref[:tokens], (0, 0))
        for i in range(1, n):
            value = value + dot(lefts[i][...], right_ref[i * tokens : (i + 1) * tokens], (0, 0))
        total[:, :right_width] = value
        if mores:
            total[:, right_width:] = total_of(mores, slice(None))
        for k in range(ng):
            at = lax.rem(g + k, ng)
            for i in range(ny):
                start = pl.multiple_of((i * ng + at) * rows, rows)
                outs[k][0, i] = half(total[pl.ds(start, rows), :columns])
        for k in range(ny):
            at = lax.rem(y + k, ny)
            for i in range(ng):
                start = pl.multiple_of((at * ng + i) * rows, rows)
                outs[ng + k][0, i] = half(total[pl.ds(start, rows), columns:])

    first = jax.ShapeDtypeStruct((nz, ny, rows, columns), BF)
    second = jax.ShapeDtypeStruct((nz, ng, rows, columns), BF)
    step = height // nz
    skip = (more[0].shape[0] - height) // step if more else 0
    outs = pl.pallas_call(
        kernel,
        grid=(nz,),
        in_specs=[whole(pltpu.SMEM)]
        + [pl.BlockSpec((tokens, step), lambda i: (0, i))] * n
        + [pl.BlockSpec((n * tokens, right_width), lambda i: (0, 0))]
        + [pl.BlockSpec((step, v.shape[1]), lambda i: (i + skip, 0)) for v in more],
        out_specs=[pl.BlockSpec((1, ny, rows, columns), lambda i: (i, 0, 0, 0))] * ng
        + [pl.BlockSpec((1, ng, rows, columns), lambda i: (i, 0, 0, 0))] * ny,
        out_shape=[first] * ng + [second] * ny,
        scratch_shapes=[pltpu.VMEM((step, width), F32)],
        compiler_params=pltpu.CompilerParams(vmem_limit_bytes=20 << 20),
        cost_estimate=cost(7),
        name="weight_grad",
    )(place, *left, right, *more)
    return outs[:ng], outs[ng:]


def total_of(refs, at):
    value = refs[0][at].astype(F32)
    for ref in refs[1:]:
        value = value + ref[at].astype(F32)
    return value


def add_split(place, sizes, first, second):
    nz, ny, ng = sizes
    rows, columns = first[0].shape[2:]

    def kernel(place_ref, *refs):
        firsts, seconds, outs = refs[:ng], refs[ng : ng + ny], refs[ng + ny :]
        y, g = place_ref[1], place_ref[2]
        for k in range(ny):
            outs[k][0] = half(total_of(firsts, (0, lax.rem(y + k, ny))))
        for k in range(ng):
            outs[ny + k][0] = half(total_of(seconds, (0, lax.rem(g + k, ng))))

    shape = jax.ShapeDtypeStruct((nz, rows, columns), BF)
    outs = pl.pallas_call(
        kernel,
        grid=(nz,),
        in_specs=[whole(pltpu.SMEM)]
        + [pl.BlockSpec((1, ny, rows, columns), lambda i: (i, 0, 0, 0))] * ng
        + [pl.BlockSpec((1, ng, rows, columns), lambda i: (i, 0, 0, 0))] * ny,
        out_specs=[pl.BlockSpec((1, rows, columns), lambda i: (i, 0, 0))] * (ny + ng),
        out_shape=[shape] * (ny + ng),
        compiler_params=pltpu.CompilerParams(vmem_limit_bytes=12 << 20),
        cost_estimate=cost(3.5),
        name="add_split",
    )(place, *[*first, *second])
    return outs[:ny], outs[ny:]


def split_over_z(first, second, more):
    ny, ng = len(first), len(second)
    nz, rows, columns = first[0].shape
    extra = [] if more is None else [more]
    count = 0 if more is None else more.shape[1]
    n_in = ny + ng + len(extra)

    def kernel(*refs):
        out = refs[n_in]
        out[0, :rows, :columns] = half(total_of(refs[:ny], 0))
        out[0, :rows, columns:] = half(total_of(refs[ny : ny + ng], 0))
        if extra:
            out[0, rows:] = half(refs[n_in - 1][0])

    return pl.pallas_call(
        kernel,
        grid=(nz,),
        in_specs=[pl.BlockSpec((1, rows, columns), lambda i: (i, 0, 0))] * (ny + ng)
        + [pl.BlockSpec((1, *m.shape[1:]), lambda i: (i, 0, 0)) for m in extra],
        out_specs=pl.BlockSpec((1, rows + count, 2 * columns), lambda i: (i, 0, 0)),
        out_shape=jax.ShapeDtypeStruct((nz, rows + count, 2 * columns), BF),
        compiler_params=pltpu.CompilerParams(vmem_limit_bytes=12 << 20),
        cost_estimate=cost(2.5),
        name="split_over_z",
    )(*first, *second, *extra)


def split_both_over_z(first, second, third, fourth):
    ny, ng = len(first), len(second)
    nz, rows, columns = first[0].shape
    high, low_columns = third[0].shape[1:]
    groups = high // rows

    def kernel(*refs):
        parts = (refs[:ny], refs[ny : ny + ng], refs[ny + ng : 2 * ny + ng], refs[2 * ny + ng : -1])
        out = refs[-1]
        for i in range(2):
            out[0, :rows, i * columns : (i + 1) * columns] = half(total_of(parts[i], 0))
            total = half(total_of(parts[2 + i], 0))
            for j in range(groups):
                start = (2 * j + i) * low_columns
                out[0, rows:, start : start + low_columns] = total[j * rows : (j + 1) * rows]

    return pl.pallas_call(
        kernel,
        grid=(nz,),
        in_specs=[pl.BlockSpec((1, rows, columns), lambda i: (i, 0, 0))] * (ny + ng)
        + [pl.BlockSpec((1, high, low_columns), lambda i: (i, 0, 0))] * (ny + ng),
        out_specs=pl.BlockSpec((1, 2 * rows, 2 * columns), lambda i: (i, 0, 0)),
        out_shape=jax.ShapeDtypeStruct((nz, 2 * rows, 2 * columns), BF),
        compiler_params=pltpu.CompilerParams(vmem_limit_bytes=12 << 20),
        cost_estimate=cost(3),
        name="split_both_over_z",
    )(*first, *second, *third, *fourth)


def send_parts(first, second, axis_first, axis_second):
    first = [first[0]] + [shift(b, axis_first, k) for k, b in enumerate(first) if k]
    second = [second[0]] + [shift(b, axis_second, k) for k, b in enumerate(second) if k]
    return first, second


def reduce_in_layer(place, sizes, parts, *others):
    first, second = parts
    first = [after(first[0], *others)] + first[1:]
    return send_parts(*add_split(place, sizes, first, second), "y", "g")


def over_z(blocks):
    return lax.all_to_all(blocks, "z", 0, 0, tiled=True)


def total_sum(blocks):
    total = blocks[0].astype(F32)
    for block in blocks[1:]:
        total = total + block.astype(F32)
    return total


def key_blocks(start, block):
    return range(max(0, start - DOC_MAX), start + block, block)


def visible_part(first_ref, low, start, block, rows, row):
    key_pos = low + row + lax.broadcasted_iota(jnp.int32, (rows, block), 0)
    visible = key_pos >= first_ref[:, start : start + block]
    if low == start:
        visible &= key_pos <= start + lax.broadcasted_iota(jnp.int32, (rows, block), 1)
    return visible


def fold(values, op):
    rows, lanes = values.shape
    return op(values.reshape(rows // 8, 8, lanes), axis=0)


def for_heads(values, head_dim):
    lane = lax.broadcasted_iota(jnp.int32, values.shape, 1) // head_dim
    heads = values.shape[1] // head_dim
    return jnp.concatenate([jnp.where(lane == h, values, jnp.zeros_like(values)) for h in range(heads)], axis=0)


def heads_of(values, head_dim, block):
    heads = values.shape[0] // head_dim
    return jnp.concatenate(
        [values[h * head_dim : (h + 1) * head_dim, h * block : (h + 1) * block] for h in range(heads)], axis=0
    )


def load_in_order(order_ref, source, into, local, columns):
    for n in range(into.shape[0] // local):
        rows = pl.ds(pl.multiple_of(order_ref[n] * local, local), local)
        into[n * local : (n + 1) * local] = source[rows, columns]


def store_in_order(order_ref, source, into, local, columns):
    for n in range(source.shape[0] // local):
        rows = pl.ds(pl.multiple_of(order_ref[n] * local, local), local)
        into[rows, columns] = half(source[n * local : (n + 1) * local])


def attend_kernel(block, sub, head_dim, local, order_ref, qkv_ref, first_ref, out_ref, log_ref, q_s, k_s, v_s, o_s, s_s):
    length, lanes = q_s.shape
    heads = lanes // head_dim
    for i, into in enumerate((q_s, k_s, v_s)):
        load_in_order(order_ref, qkv_ref, into, local, slice(i * lanes, (i + 1) * lanes))
    v_t = v_s[...].T
    for start in range(0, length, block):
        q_heads = for_heads(q_s[start : start + block] * (head_dim ** (-0.5)), head_dim)
        lows = list(key_blocks(start, block))
        top8 = [jnp.full((8, block), -1e30, F32)] * heads
        for n, low in enumerate(lows):
            scores = dot(k_s[low : low + block], q_heads, (1, 1))
            for r in range(0, block, sub):
                visible = visible_part(first_ref, low, start, block, sub, r)
                rows = slice(n * block + r, n * block + r + sub)
                for h in range(heads):
                    columns = slice(h * block, (h + 1) * block)
                    piece = jnp.where(visible, scores[r : r + sub, columns], -1e30)
                    top8[h] = jnp.maximum(top8[h], fold(piece, jnp.max))
                    s_s[rows, columns] = piece
        width = len(lows) * block
        top = jnp.concatenate([jnp.max(v, axis=0, keepdims=True) for v in top8], axis=1)
        total8 = jnp.zeros((8, heads * block), F32)
        for r in range(0, width, sub):
            exponent = jnp.exp(s_s[r : r + sub] - top)
            total8 = total8 + fold(exponent, jnp.sum)
            s_s[r : r + sub] = exponent
        total = jnp.sum(total8, axis=0, keepdims=True)
        probs = half(s_s[:width] * (1.0 / total))
        out = dot(v_t[:, lows[0] : lows[0] + width], probs, (1, 0))
        log = top + jnp.log(total)
        for h in range(heads):
            log_ref[0, h : h + 1, start : start + block] = log[:, h * block : (h + 1) * block]
        o_s[start : start + block] = half(heads_of(out, head_dim, block).T)
    store_in_order(order_ref, o_s, out_ref, local, slice(None))


def attend_back_kernel(
    block,
    sub,
    head_dim,
    local,
    order_ref,
    qkv_ref,
    g_refs,
    log_ref,
    first_ref,
    out_ref,
    sum_ref,
    q_s,
    k_s,
    v_s,
    g_s,
    g_raw,
    query_grad,
    key_sum,
    value_sum,
    p_s,
    d_s,
):
    length, lanes = q_s.shape
    heads = lanes // head_dim
    scale = head_dim ** (-0.5)
    for i, into in enumerate((q_s, k_s, v_s)):
        load_in_order(order_ref, qkv_ref, into, local, slice(i * lanes, (i + 1) * lanes))
    own = g_refs[0].shape[0]
    for i, ref in enumerate(g_refs):
        g_raw[i * own : (i + 1) * own] = ref[...]
    load_in_order(order_ref, g_raw, g_s, local, slice(None))
    k_t = k_s[...].T
    for start in range(0, length, block):
        q_heads = for_heads(q_s[start : start + block] * scale, head_dim)
        g_heads = for_heads(g_s[start : start + block], head_dim)
        lows = list(key_blocks(start, block))
        delta8 = [jnp.zeros((8, block), F32)] * heads
        for n, low in enumerate(lows):
            scores = dot(k_s[low : low + block], q_heads, (1, 1))
            grads = dot(v_s[low : low + block], g_heads, (1, 1))
            for r in range(0, block, sub):
                visible = visible_part(first_ref, low, start, block, sub, r)
                rows = slice(n * block + r, n * block + r + sub)
                for h in range(heads):
                    columns = slice(h * block, (h + 1) * block)
                    p = jnp.where(visible, scores[r : r + sub, columns], -1e30)
                    p = jnp.exp(p - log_ref[0, h : h + 1, start : start + block])
                    d = grads[r : r + sub, columns]
                    delta8[h] = delta8[h] + fold(p * d, jnp.sum)
                    p_s[rows, columns] = p
                    d_s[rows, columns] = d
        delta = jnp.concatenate([jnp.sum(v, axis=0, keepdims=True) for v in delta8], axis=1)
        width = len(lows) * block
        p = p_s[:width]
        grad_scores = half(p * (d_s[:width] - delta))
        dq = dot(k_t[:, lows[0] : lows[0] + width], grad_scores, (1, 0))
        dk = dot(grad_scores, q_heads, (1, 0))
        dv = dot(half(p), g_heads, (1, 0))
        for n, low in enumerate(lows):
            rows = slice(n * block, (n + 1) * block)
            if low == start:
                key_sum[low : low + block] = dk[rows]
                value_sum[low : low + block] = dv[rows]
            else:
                key_sum[low : low + block] += dk[rows]
                value_sum[low : low + block] += dv[rows]
        query_grad[start : start + block] = (heads_of(dq, head_dim, block) * scale).T
    for i, source in enumerate((query_grad, key_sum, value_sum)):
        columns = slice(i * lanes, (i + 1) * lanes)
        store_in_order(order_ref, source, out_ref, local, columns)
        sum_ref[:, columns] = jnp.sum(half(source[...]).astype(F32), axis=0, keepdims=True)


def attend(qkv, first, order, local, head_dim):
    length, width = qkv.shape
    block = min(256, length)
    window = min(length, DOC_MAX + block)
    lanes = 2 * head_dim
    steps = width // (3 * lanes)

    def kernel(*refs):
        attend_kernel(block, 64, head_dim, local, *refs)

    return pl.pallas_call(
        kernel,
        grid=(steps,),
        in_specs=[
            whole(pltpu.SMEM),
            pl.BlockSpec((length, 3 * lanes), lambda i: (0, i)),
            pl.BlockSpec((1, length), lambda i: (0, 0)),
        ],
        out_specs=[
            pl.BlockSpec((length, lanes), lambda i: (0, i)),
            pl.BlockSpec((1, 2, length), lambda i: (i, 0, 0)),
        ],
        out_shape=[
            jax.ShapeDtypeStruct((length, width // 3), BF),
            jax.ShapeDtypeStruct((steps, 2, length), F32),
        ],
        scratch_shapes=[pltpu.VMEM((length, lanes), BF)] * 4 + [pltpu.VMEM((window, 2 * block), F32)],
        compiler_params=pltpu.CompilerParams(vmem_limit_bytes=16 << 20),
        cost_estimate=cost(11.5 * steps / 4),
        name="attend",
    )(order, qkv, first[None])


def attend_back(qkv, grad_out, logs, first, order, local, head_dim):
    length, width = qkv.shape
    block = min(256, length)
    window = min(length, DOC_MAX + block)
    lanes = 2 * head_dim
    steps = width // (3 * lanes)

    n = len(grad_out)
    own = length // n

    def kernel(order_ref, qkv_ref, *refs):
        attend_back_kernel(block, 64, head_dim, local, order_ref, qkv_ref, refs[:n], *refs[n:])

    return pl.pallas_call(
        kernel,
        grid=(steps,),
        in_specs=[
            whole(pltpu.SMEM),
            pl.BlockSpec((length, 3 * lanes), lambda i: (0, i)),
        ]
        + [pl.BlockSpec((own, lanes), lambda i: (0, i))] * n
        + [
            pl.BlockSpec((1, 2, length), lambda i: (i, 0, 0)),
            pl.BlockSpec((1, length), lambda i: (0, 0)),
        ],
        out_specs=[
            pl.BlockSpec((length, 3 * lanes), lambda i: (0, i)),
            pl.BlockSpec((1, 3 * lanes), lambda i: (0, i)),
        ],
        out_shape=[jax.ShapeDtypeStruct((length, width), BF), jax.ShapeDtypeStruct((1, width), F32)],
        scratch_shapes=[pltpu.VMEM((length, lanes), BF)] * 5
        + [pltpu.VMEM((length, lanes), F32)] * 3
        + [pltpu.VMEM((window, 2 * block), F32)] * 2,
        compiler_params=pltpu.CompilerParams(vmem_limit_bytes=20 << 20),
        cost_estimate=cost(18 * steps / 4),
        name="attend_back",
    )(order, qkv, *grad_out, logs, first[None])


def product(left, right, contract, kind, bias=None, rows=None, part=0):
    rows = left.shape[0] if rows is None else rows
    depth = left.shape[1]
    width = right.shape[1 - contract[1]]
    block = min(256, width)
    extra = [] if bias is None else [bias[None]]

    def kernel(left_ref, right_ref, *refs):
        out = dot(left_ref[...], right_ref[...], contract)
        if extra:
            out = out + refs[0][...]
        refs[-1][...] = out.astype(kind)

    if contract[1] == 0:
        right_spec = pl.BlockSpec((depth, block), lambda i: (0, i))
    else:
        right_spec = pl.BlockSpec((block, depth), lambda i: (i, 0))
    return pl.pallas_call(
        kernel,
        grid=(width // block,),
        in_specs=[pl.BlockSpec((rows, depth), lambda i: (part, 0)), right_spec]
        + [pl.BlockSpec((1, block), lambda i: (0, i)) for _ in extra],
        out_specs=pl.BlockSpec((rows, block), lambda i: (0, i)),
        out_shape=jax.ShapeDtypeStruct((rows, width), kind),
        compiler_params=pltpu.CompilerParams(vmem_limit_bytes=16 << 20),
        cost_estimate=cost(2.3 * rows * width * depth / 2**30),
        name="product",
    )(left, right, *extra)


def norm_back_part(summands, values, gain, added, scale=None):
    tokens, width = values.shape
    block = min(128, tokens)
    n = len(summands)

    def kernel(*refs):
        ins, outs = refs[: n + 3], refs[n + 3 :]

        @pl.when(pl.program_id(0) == 0)
        def _():
            for ref in outs[1 if scale is None else 2 :]:
                ref[...] = jnp.zeros_like(ref)

        grad = ins[0][...].astype(F32)
        for ref in ins[1:n]:
            grad = grad + ref[...].astype(F32)
        normal, inverse = norm_parts(ins[n][...].astype(F32))
        out = ins[n + 2][...].astype(F32) + norm_back(grad, normal, inverse, ins[n + 1][...])
        sums = [grad * normal, grad]
        if scale is None:
            outs[0][...] = half(out)
            rest = outs[1:]
        else:
            outs[0][...] = out
            scaled = half(scale * out)
            outs[1][...] = scaled
            sums.append(scaled.astype(F32))
            rest = outs[2:]
        for ref, value in zip(rest, sums):
            ref[...] += jnp.sum(value, axis=0, keepdims=True)

    row = pl.BlockSpec((block, width), lambda i: (i, 0))
    one = pl.BlockSpec((1, width), lambda i: (0, 0))
    total = jax.ShapeDtypeStruct((1, width), F32)
    if scale is None:
        out_specs, out_shape = [row, one, one], [jax.ShapeDtypeStruct((tokens, width), BF), total, total]
    else:
        out_specs = [row, row, one, one, one]
        out_shape = [
            jax.ShapeDtypeStruct((tokens, width), F32),
            jax.ShapeDtypeStruct((tokens, width), BF),
            total,
            total,
            total,
        ]
    return pl.pallas_call(
        kernel,
        grid=(tokens // block,),
        in_specs=[row] * n + [row, one, row],
        out_specs=out_specs,
        out_shape=out_shape,
        compiler_params=pltpu.CompilerParams(vmem_limit_bytes=16 << 20),
        cost_estimate=cost(3),
        name="norm_back_part",
    )(*summands, values, gain[None], added)


def proj_norm(here, parts, weights, bias, gain, shift_by, x, depth):
    nt = len(parts)
    tokens, width = x.shape
    part = width // nt
    block = min(128, tokens)

    def kernel(here_ref, *refs):
        parts_in, weights_in = refs[:nt], refs[nt : 2 * nt]
        bias_ref, gain_ref, shift_ref, x_ref, hidden_ref, normed_ref = refs[2 * nt :]
        t = here_ref[0]
        for j in range(nt):
            total = 0.0
            for k in range(nt):
                rows = pl.ds(pl.multiple_of(lax.rem(t + k, nt) * part, part), part)
                total = total + dot(parts_in[k][...], weights_in[j][rows, :], (1, 0))
            columns = pl.ds(pl.multiple_of(lax.rem(t - j + nt, nt) * part, part), part)
            hidden_ref[:, columns] = x_ref[:, columns].astype(F32) + depth * (total + bias_ref[:, columns])
        normal, _ = norm_parts(hidden_ref[...])
        normed_ref[...] = half(normal * gain_ref[...] + shift_ref[...])

    row = pl.BlockSpec((block, width), lambda i: (i, 0))
    one = pl.BlockSpec((1, width), lambda i: (0, 0))
    return pl.pallas_call(
        kernel,
        grid=(tokens // block,),
        in_specs=[whole(pltpu.SMEM)]
        + [pl.BlockSpec((block, part), lambda i: (i, 0))] * nt
        + [pl.BlockSpec((width, part), lambda i: (0, 0))] * nt
        + [one, one, one, row],
        out_specs=[row, row],
        out_shape=[jax.ShapeDtypeStruct((tokens, width), F32), jax.ShapeDtypeStruct((tokens, width), BF)],
        compiler_params=pltpu.CompilerParams(vmem_limit_bytes=16 << 20),
        cost_estimate=cost(3),
        name="proj_norm",
    )(here, *parts, *weights, bias[None], gain[None], shift_by[None], x)


def proj_back(here, grad, parts, weights):
    nt = len(parts)
    tokens, width = grad.shape
    part = width // nt

    def kernel(here_ref, grad_ref, *refs):
        parts_in, weights_in, outs = refs[:nt], refs[nt : 2 * nt], refs[2 * nt :]
        t = here_ref[0]

        def place(step, offset=0):
            return pl.ds(pl.multiple_of(lax.rem(t + step + nt, nt) * part + offset, 128), part)

        for k in range(nt):
            total = 0.0
            for j in range(nt):
                total = total + dot(grad_ref[:, place(-j)], weights_in[j][place(k), :], (1, 1))
            outs[k][:tokens] = half(total)
        for k in range(nt):
            for m in range(nt):
                outs[k][place(m, tokens), :] = half(dot(parts_in[m][...], grad_ref[:, place(k)], (0, 0)))

    return pl.pallas_call(
        kernel,
        in_specs=[whole(pltpu.SMEM)] + [whole()] * (1 + 2 * nt),
        out_specs=[whole()] * nt,
        out_shape=[jax.ShapeDtypeStruct((tokens + width, part), BF)] * nt,
        compiler_params=pltpu.CompilerParams(vmem_limit_bytes=24 << 20),
        cost_estimate=cost(4),
        name="proj_back",
    )(here, grad, *parts, *weights)


def gelu_parts(u):
    c = 0.7978845608028654
    square = u * u
    h = 0.5 + 0.5 * jnp.tanh(u * (c + (c * 0.044715) * square))
    value = u * h
    return value, h + value * (1.0 - h) * (2 * c + (6 * c * 0.044715) * square)


def up_part(normed, weight, bias):
    n = len(normed)
    tokens, width = normed[0].shape
    ff = weight.shape[1]
    block = min(256, ff)
    rows = min(512, tokens)

    def kernel(*refs):
        w_ref, b_ref, active_ref, slope_ref = refs[n:]
        for i in range(n):
            for r in range(0, tokens, rows):
                u = dot(refs[i][r : r + rows], w_ref[...], (1, 0)) + b_ref[...]
                value, slope = gelu_parts(u)
                at = slice(i * tokens + r, i * tokens + r + rows)
                active_ref[at] = half(value)
                slope_ref[at] = slope

    column = pl.BlockSpec((n * tokens, block), lambda i: (0, i))
    return pl.pallas_call(
        kernel,
        grid=(ff // block,),
        in_specs=[pl.BlockSpec((tokens, width), lambda i: (0, 0))] * n
        + [
            pl.BlockSpec((width, block), lambda i: (0, i)),
            pl.BlockSpec((1, block), lambda i: (0, i)),
        ],
        out_specs=[column, column],
        out_shape=[jax.ShapeDtypeStruct((n * tokens, ff), BF), jax.ShapeDtypeStruct((n * tokens, ff), F32)],
        compiler_params=pltpu.CompilerParams(vmem_limit_bytes=16 << 20),
        cost_estimate=cost(7),
        name="up_part",
    )(*normed, weight, bias[None])


def up_back(grad_down, weight, slope):
    tokens, width = grad_down.shape
    ff = weight.shape[0]
    block = min(256, ff)
    rows = min(512, tokens)

    def kernel(g_ref, w_ref, slope_ref, out_ref, sum_ref):
        total = jnp.zeros((8, block), F32)
        for r in range(0, tokens, rows):
            grad = half(dot(g_ref[r : r + rows], w_ref[...], (1, 1)) * slope_ref[r : r + rows])
            out_ref[r : r + rows] = grad
            total = total + fold(grad.astype(F32), jnp.sum)
        sum_ref[...] = jnp.sum(total, axis=0, keepdims=True)

    column = pl.BlockSpec((tokens, block), lambda i: (0, i))
    return pl.pallas_call(
        kernel,
        grid=(ff // block,),
        in_specs=[
            pl.BlockSpec((tokens, width), lambda i: (0, 0)),
            pl.BlockSpec((block, width), lambda i: (i, 0)),
            column,
        ],
        out_specs=[column, pl.BlockSpec((1, block), lambda i: (0, i))],
        out_shape=[jax.ShapeDtypeStruct((tokens, ff), BF), jax.ShapeDtypeStruct((1, ff), F32)],
        compiler_params=pltpu.CompilerParams(vmem_limit_bytes=16 << 20),
        cost_estimate=cost(6.5),
        name="up_back",
    )(*[grad_down, weight, slope])


def body(
    block_input,
    doc_ids,
    gain_attn,
    shift_attn,
    w_qkv,
    bias_qv,
    w_proj,
    bias_proj,
    gain_mlp,
    shift_mlp,
    w_up,
    bias_up,
    w_down,
    bias_down,
    out_grad,
):
    nz, ny, ng, nt = (lax.axis_size(a) for a in ("z", "y", "g", "t"))
    sizes = (nz, ny, ng)
    z, y, g, t = (lax.axis_index(a) for a in ("z", "y", "g", "t"))
    place = jnp.stack([z, y, g]).astype(jnp.int32)
    chips = nz * ny * ng
    depth = LAYERS ** (-0.5)
    _, local, width = block_input.shape
    length = doc_ids.shape[1]
    shard = w_qkv.shape[0]
    part = width // nt
    head_dim = width // H
    lanes = 2 * head_dim
    pairs = part // lanes
    hidden_width = w_up.shape[1]
    ff_shard = w_down.shape[0]
    ff_part = hidden_width // nt
    own = ng * local
    block_rows = nt * shard

    natural = jnp.arange(ng * nt, dtype=jnp.int32)
    order = lax.rem(t - natural % nt + nt, nt) * ng + lax.rem(g - natural // nt + ng, ng)
    docs = lax.dynamic_index_in_dim(doc_ids, g, 0, keepdims=False)
    first_token = jnp.sum((docs[None, :] < docs[:, None]).astype(jnp.int32), axis=1)

    both = jnp.stack([block_input, out_grad], axis=1)
    parts = []
    for k in range(ng):
        block = lax.dynamic_index_in_dim(both, lax.rem(g + k, ng), 0, keepdims=False)
        parts.append(shift(block, "g", k) if k else block)
    both_own = jnp.concatenate(parts, axis=1)
    x_own, grad_own = both_own[0], both_own[1]
    both_all = jnp.concatenate(gather_relative(both_own, "t"), axis=1)

    vectors = [gain_attn, shift_attn, bias_qv, bias_proj, gain_mlp, shift_mlp, bias_up, bias_down]
    counts = [v.shape[0] for v in vectors]
    packed = half(lax.optimization_barrier(jnp.concatenate(vectors)))
    count = packed.shape[0]
    columns_a = half(w_qkv).reshape(shard, 3, nt, pairs, lanes).transpose(2, 0, 3, 1, 4).reshape(nt, shard, 3 * part)
    columns_o = half(w_proj).reshape(shard, nt, part).transpose(1, 0, 2)
    columns_u = half(w_up).reshape(shard, chips, nt, ff_shard).transpose(2, 0, 1, 3).reshape(nt, shard, ff_part)
    columns = jnp.concatenate([columns_a, columns_o, columns_u], axis=2)
    wide = columns.shape[2]
    packed = jnp.broadcast_to(jnp.pad(packed, (0, wide - count)), (nt, 8, wide))
    columns = swap_axis(jnp.concatenate([columns, packed], axis=1), "t", 0)
    packed = jnp.concatenate([c[shard : shard + 1, :count] for c in columns], axis=1)
    columns = jnp.concatenate([c[:shard] for c in columns], axis=0)
    packed = jnp.broadcast_to(jnp.pad(packed, ((0, 0), (0, 4 * part - nt * count))), (8, 4 * part))
    shard_a = jnp.concatenate([columns[:, : 4 * part], packed], axis=0)
    shard_u = columns[:, 4 * part :]
    shard_d = half(w_down)
    middle_d = width // 2

    first_d, second_d = gather_once(shard_d[:, :middle_d], shard_d[:, middle_d:])
    first_a, second_a = halves(gather_over_z(after(shard_a, first_d, second_d)))
    first_u, second_u = halves(gather_over_z(after(shard_u, first_a, second_a)))
    first_a, second_a = gather_once(first_a, second_a)
    both_d = jnp.concatenate([first_d, second_d], axis=0)
    both_d = gather_over_z(after(both_d, first_u, second_u, first_a, second_a))
    first_a, second_a = gather_twice(first_a, second_a)
    side = 3 * part - 2 * part
    wqkv, wo, vector_rows = assemble(
        place,
        first_a,
        second_a,
        [
            [(0, 0, block_rows, 0, 2 * part, 0), (1, 0, block_rows, 0, side, 2 * part)],
            [(1, 0, block_rows, side, part, 0)],
            [(0, block_rows, 8, 0, 2 * part, 0)],
        ],
        [(block_rows, 3 * part), (block_rows, part), (8, 2 * part)],
    )
    wqkv = wqkv.reshape(width, 3 * part)
    wo = wo.reshape(width, part)
    first_u, second_u = gather_once(after(first_u, *first_a, *second_a), after(second_u, *first_a, *second_a))

    vector_rows = vector_rows.reshape(chips, 8, 2 * part)[:, 0, : nt * count].reshape(chips, nt, count)
    offsets = [0]
    for size in counts:
        offsets.append(offsets[-1] + size)
    pieces = [vector_rows[:, :, offsets[i] : offsets[i + 1]] for i in range(len(counts))]
    h_gain_attn, h_shift_attn, h_bias_qv, h_bias_proj, h_gain_mlp, h_shift_mlp = (
        p.reshape(-1).astype(F32) for p in pieces[:6]
    )
    h_bias_down = pieces[7].reshape(-1).astype(F32)
    h_bias_up = lax.dynamic_index_in_dim(pieces[6], t, 1, keepdims=False).astype(F32).reshape(-1)
    bias_q = lax.dynamic_slice_in_dim(h_bias_qv, t * part, part).reshape(pairs, lanes)
    bias_v = lax.dynamic_slice_in_dim(h_bias_qv, width + t * part, part).reshape(pairs, lanes)
    bias_qkv = jnp.stack([bias_q, jnp.zeros_like(bias_q), bias_v], axis=1).reshape(-1)

    normal_all, _ = norm_parts(both_all[0].astype(F32))
    normed_attn = half(normal_all * h_gain_attn + h_shift_attn)
    grad_down = half(depth * both_all[1].astype(F32))
    d_bias_down = jnp.sum(grad_down[:own], axis=0, dtype=F32)
    normed_attn = after(normed_attn, d_bias_down)
    qkv = product(normed_attn, wqkv, (1, 0), BF, bias_qkv)
    qkv = after(qkv, first_u, second_u)
    attended_heads, logs = attend(qkv, first_token, order, local, head_dim)
    first_u, second_u = gather_twice(first_u, second_u)
    wo_parts = gather_relative(wo, "t")
    attended_parts = return_relative([attended_heads[k * own : (k + 1) * own] for k in range(nt)], "t")
    here = t.astype(jnp.int32)[None]
    hidden, normed_own = proj_norm(
        here,
        attended_parts,
        wo_parts,
        h_bias_proj,
        h_gain_mlp,
        h_shift_mlp,
        after(x_own, *first_u, *second_u),
        depth,
    )
    normed_mlp = gather_relative(normed_own, "t")
    (wu,) = assemble(
        place,
        first_u,
        second_u,
        [[(0, 0, block_rows, 0, ff_part // 2, 0), (1, 0, block_rows, 0, ff_part // 2, ff_part // 2)]],
        [(block_rows, ff_part)],
    )
    wu = wu.reshape(width, ff_part)
    first_d, second_d = both_d[:, :ng].swapaxes(0, 1), both_d[:, ng:].swapaxes(0, 1)
    first_d, second_d = gather_twice(after(first_d, *first_u, *second_u), after(second_d, *first_u, *second_u))
    active, slope = up_part(normed_mlp, wu, h_bias_up)

    def own_sum(left, right, contract):
        blocks = [product(left, right, contract, BF, rows=own, part=k) for k in range(1, nt)]
        mine = product(after(left, *blocks), right, contract, F32, rows=own)
        return [mine] + [shift(block, "t", -k - 1) for k, block in enumerate(blocks)]

    down_blocks = weight_grad(place, sizes, [active], grad_down)
    down_parts = send_parts(*down_blocks, "g", "y")
    (wd,) = assemble(
        place,
        first_d,
        second_d,
        [[(0, 0, ff_shard, 0, middle_d, 0), (1, 0, ff_shard, 0, middle_d, middle_d)]],
        [(ff_shard, width)],
    )
    wd = wd.reshape(ff_part, width)
    grad_up, d_bias_up = up_back(after(grad_down, *down_blocks[0]), wd, slope)
    up_blocks = weight_grad(place, sizes, normed_mlp, grad_up)
    down_parts = reduce_in_layer(place, sizes, down_parts, *up_blocks[0])
    up_parts = send_parts(*up_blocks, "g", "y")
    e2 = own_sum(after(grad_up, up_blocks[0][0]), wu, (1, 1))

    grad_hidden, grad_branch, d_gain_mlp, d_shift_mlp, d_bias_proj = norm_back_part(
        e2, after(hidden, down_parts[0][0]), h_gain_mlp, grad_own, depth
    )


    def to_rows(blocks):
        return jnp.stack(by_place(return_relative([blocks[k] for k in range(ng)], "g"), "g", 1), axis=0)

    lowered = own_sum(after(active, grad_branch), wd, (1, 0))
    up_parts = reduce_in_layer(place, sizes, up_parts, lowered[0])
    back_parts = proj_back(here, after(grad_branch, up_parts[0][0]), attended_parts, wo_parts)
    back_parts = [back_parts[0]] + [shift(b, "t", k) for k, b in enumerate(back_parts) if k]
    block_out = half(hidden + depth * (total_sum(lowered) + h_bias_down)).reshape(ng, local, width)
    grad_attended = [after(b, block_out) for b in back_parts]

    def to_rows(blocks):
        return jnp.stack(by_place(return_relative([blocks[k] for k in range(ng)], "g"), "g", 1), axis=0)

    d_qkv, d_bias_qkv = attend_back(qkv, grad_attended, logs, first_token, order, local, head_dim)
    a_blocks = weight_grad(place, sizes, [normed_attn], d_qkv, back_parts)
    a_parts = send_parts(*a_blocks, "g", "y")
    d_qkv = after(d_qkv, *a_blocks[0])
    both_split = split_both_over_z([after(up_parts[0][0], d_qkv)] + up_parts[0][1:], up_parts[1], *down_parts)
    both_sent = over_z(both_split)
    d_qkv = after(d_qkv, both_split)
    e1 = own_sum(d_qkv, wqkv, (1, 1))
    grad_input, d_gain_attn, d_shift_attn = norm_back_part(e1, x_own, h_gain_attn, grad_hidden)
    def by_owner(full):
        return full.reshape(chips, nt, -1)

    d_bias_qkv = d_bias_qkv.reshape(pairs, 3, lanes)
    d_bias_qv = jnp.zeros((2 * width,), F32)
    d_bias_qv = lax.dynamic_update_slice_in_dim(d_bias_qv, d_bias_qkv[:, 0].reshape(-1), t * part, 0)
    d_bias_qv = lax.dynamic_update_slice_in_dim(d_bias_qv, d_bias_qkv[:, 2].reshape(-1), width + t * part, 0)
    d_bias_up = d_bias_up.reshape(chips, 1, ff_shard)
    d_bias_up = jnp.where(lax.broadcasted_iota(jnp.int32, (chips, nt, 1), 1) == t, d_bias_up, 0.0)
    sums = jnp.concatenate(
        [
            by_owner(d_gain_attn),
            by_owner(d_shift_attn),
            by_owner(d_bias_qv),
            by_owner(d_bias_proj),
            by_owner(d_gain_mlp),
            by_owner(d_shift_mlp),
            d_bias_up,
            by_owner(d_bias_down),
        ],
        axis=2,
    )
    sums = sums.reshape(nz, ny * ng, nt * count)
    a_parts = reduce_in_layer(place, sizes, a_parts, sums)
    sums = reduce_axes(sums, ("y", "g"), 1)
    high = half(sums)
    more = jnp.stack([high.astype(F32), sums - high.astype(F32)], axis=1)
    more = jnp.pad(more, ((0, 0), (0, 6), (0, 4 * part - nt * count)))
    a_blocks = split_over_z(*a_parts, after(more, both_sent))
    block_out = to_rows(after(block_out, a_blocks))
    grad_input = to_rows(after(grad_input, a_blocks).reshape(ng, local, width)).astype(F32)
    both = jnp.sum(after(both_sent, a_blocks).astype(F32), axis=0)
    sum_up = both[:block_rows]
    sum_down = jnp.concatenate(jnp.split(both[block_rows:], ff_part // width, axis=1), axis=0)
    sum_a = jnp.sum(over_z(a_blocks).astype(F32), axis=0)
    sums = (sum_a[block_rows, : nt * count] + sum_a[block_rows + 1, : nt * count]).reshape(nt, 1, count)
    sums = jnp.pad(sums, ((0, 0), (0, 7), (0, 4 * part - count)))
    rest = jnp.concatenate([sum_a[:block_rows].reshape(nt, shard, 4 * part), sums], axis=1)
    rest = swap_axis(rest, "t", 0)
    sums = total_sum([r[shard, :count] for r in rest])
    rest = [r[:shard] for r in rest]
    out_vectors = [sums[offsets[i] : offsets[i + 1]] for i in range(len(counts))]

    up = swap_axis(sum_up.reshape(nt, shard, ff_part), "t", 0)
    sum_up = jnp.stack([u.reshape(shard, chips, ff_shard) for u in up], axis=2).reshape(shard, hidden_width)
    sum_qkv = jnp.stack([r[:, : 3 * part].reshape(shard, pairs, 3, lanes) for r in rest], axis=1)
    sum_qkv = sum_qkv.transpose(0, 3, 1, 2, 4).reshape(shard, 3 * width)
    sum_proj = jnp.concatenate([r[:, 3 * part :] for r in rest], axis=1)
    return (
        block_out,
        grad_input,
        out_vectors[0],
        out_vectors[1],
        sum_qkv,
        out_vectors[2],
        sum_proj,
        out_vectors[3],
        out_vectors[4],
        out_vectors[5],
        sum_up,
        out_vectors[6],
        sum_down,
        out_vectors[7],
    )


def solution(mesh):
    rows = 2
    dp, seq = mesh.shape["dp"], mesh.shape["seq"]
    high = 4
    split = Mesh(mesh.devices.reshape(high, dp // high, rows, seq // rows), ("z", "y", "g", "t"))
    everything = ("z", "y", "g", "t")
    tokens = P(("z", "y"), ("g", "t"), None)
    vector = P(everything)
    matrix = P(everything, None)
    return jax.shard_map(
        body,
        mesh=split,
        in_specs=(
            tokens,
            P(("z", "y"), None),
            vector,
            vector,
            matrix,
            vector,
            matrix,
            vector,
            vector,
            vector,
            matrix,
            vector,
            matrix,
            vector,
            tokens,
        ),
        out_specs=(
            tokens,
            tokens,
            vector,
            vector,
            matrix,
            vector,
            matrix,
            vector,
            vector,
            vector,
            matrix,
            vector,
            matrix,
            vector,
        ),
        check_vma=False,
    )
```

```python
import jax
import jax.numpy as jnp
from jax import lax
from jax.experimental import pallas as pl
from jax.experimental.pallas import tpu as pltpu
from jax.sharding import Mesh, PartitionSpec as P

H = 16
LAYERS = 24
EPSILON = 1e-05
DOC_MAX = 512

BF = jnp.bfloat16
F32 = jnp.float32


def half(values):
    return values.astype(BF)


def norm_parts(values):
    mean = jnp.mean(values, axis=-1, keepdims=True)
    centred = values - mean
    spread = jnp.mean(centred * centred, axis=-1, keepdims=True)
    inverse = lax.rsqrt(spread + EPSILON)
    return (centred * inverse, inverse)


def norm_back(grad_out, normal, inverse, gain):
    scaled = grad_out * gain
    return inverse * (
        scaled
        - jnp.mean(scaled, axis=-1, keepdims=True)
        - normal * jnp.mean(scaled * normal, axis=-1, keepdims=True)
    )


def dot(left, right, contract):
    return lax.dot_general(left, right, ((contract[:1], contract[1:]), ((), ())), preferred_element_type=F32)


def cost(microseconds):
    return pl.CostEstimate(flops=int(microseconds * 0.9e8), bytes_accessed=int(microseconds * 0.3e6), transcendentals=0)


def after(value, *others):
    return lax.optimization_barrier((value, *others))[0]


def shift(value, axis, step):
    size = lax.axis_size(axis)
    return lax.ppermute(value, axis, [(i, (i + step) % size) for i in range(size)])


def gather_relative(value, axis):
    return [value] + [shift(value, axis, k) for k in range(1, lax.axis_size(axis))]


def return_relative(blocks, axis):
    return [blocks[0]] + [shift(block, axis, -k) for k, block in enumerate(blocks) if k]


def by_place(parts, axis, sign):
    size = len(parts)
    here = lax.axis_index(axis)
    return [lax.select_n(lax.rem(sign * (place - here) + size, size), *parts) for place in range(size)]


def swap_axis(value, axis, at):
    size = lax.axis_size(axis)
    here = lax.axis_index(axis)
    parts = []
    for k in range(size):
        block = lax.dynamic_index_in_dim(value, lax.rem(here + k, size), at, keepdims=False)
        parts.append(shift(block, axis, k) if k else block)
    return by_place(parts, axis, -1)


def reduce_axes(value, axes, at):
    size = 1
    for axis in axes:
        size = size * lax.axis_size(axis)
    here = lax.axis_index(axes)
    total = lax.dynamic_index_in_dim(value, here, at, keepdims=False)
    for k in range(1, size):
        block = lax.dynamic_index_in_dim(value, lax.rem(here + k, size), at, keepdims=False)
        total = total + lax.ppermute(block, axes, [(i, (i + k) % size) for i in range(size)])
    return total


def reduce_axis(value, axis, at):
    size = lax.axis_size(axis)
    here = lax.axis_index(axis)
    total = lax.dynamic_index_in_dim(value, here, at, keepdims=False)
    for k in range(1, size):
        block = lax.dynamic_index_in_dim(value, lax.rem(here + k, size), at, keepdims=False)
        total = total + shift(block, axis, k)
    return total


def whole(memory_space=pltpu.VMEM):
    return pl.BlockSpec(memory_space=memory_space)


def assemble(place, firsts, seconds, wanted, shapes):
    ny, ng = len(firsts), len(seconds)
    nz, high, wide = firsts[0].shape[1:]

    def kernel(place_ref, *refs):
        ins, outs = (refs[:ny], refs[ny : ny + ng]), refs[ny + ng :]
        y, g = place_ref[1], place_ref[2]
        for pieces, out in zip(wanted, outs):
            for which, row, rows, column, columns, into in pieces:
                for ky in range(ny):
                    for kg in range(ng):
                        source = ins[0][ky].at[kg, 0] if which == 0 else ins[1][kg].at[ky, 0]
                        at = (0, lax.rem(y - ky + ny, ny), lax.rem(g - kg + ng, ng))
                        out[(*at, slice(None), pl.ds(into, columns))] = source[row : row + rows, column : column + columns]

    def out_spec(shape):
        return pl.BlockSpec((1, ny, ng, *shape), lambda i, place_ref: (i, 0, 0, 0, 0))

    return pl.pallas_call(
        kernel,
        grid_spec=pltpu.PrefetchScalarGridSpec(
            num_scalar_prefetch=1,
            grid=(nz,),
            in_specs=[pl.BlockSpec((ng, 1, high, wide), lambda i, place_ref: (0, i, 0, 0))] * ny
            + [pl.BlockSpec((ny, 1, high, wide), lambda i, place_ref: (0, i, 0, 0))] * ng,
            out_specs=[out_spec(shape) for shape in shapes],
        ),
        out_shape=[jax.ShapeDtypeStruct((nz, ny, ng, *shape), BF) for shape in shapes],
        compiler_params=pltpu.CompilerParams(vmem_limit_bytes=16 << 20),
        cost_estimate=cost(4),
        name="assemble",
    )(place, *[*firsts, *seconds])


def gather_over_z(value):
    copies = jnp.broadcast_to(value[None], (lax.axis_size("z"), *value.shape))
    return lax.all_to_all(copies, "z", 0, 0, tiled=True)


def halves(values):
    middle = values.shape[-1] // 2
    return values[..., :middle], values[..., middle:]


def gather_once(first, second):
    return jnp.stack(gather_relative(first, "g")), jnp.stack(gather_relative(second, "y"))


def gather_twice(first, second):
    return gather_relative(first, "y"), gather_relative(second, "g")


def weight_grad(place, sizes, left, right, more=()):
    nz, ny, ng = sizes
    n, m = len(left), len(more)
    tokens, height = left[0].shape
    right_width = right.shape[1]
    width = right_width + (more[0].shape[1] if more else 0)
    rows, columns = height // (nz * ny * ng), width // 2

    def kernel(place_ref, *refs):
        lefts, right_ref, mores, outs, total = refs[:n], refs[n], refs[n + 1 : n + 1 + m], refs[n + 1 + m : -1], refs[-1]
        y, g = place_ref[1], place_ref[2]
        value = dot(lefts[0][...], right_ref[:tokens], (0, 0))
        for i in range(1, n):
            value = value + dot(lefts[i][...], right_ref[i * tokens : (i + 1) * tokens], (0, 0))
        total[:, :right_width] = value
        if mores:
            total[:, right_width:] = total_of(mores, slice(None))
        for k in range(ng):
            at = lax.rem(g + k, ng)
            for i in range(ny):
                start = pl.multiple_of((i * ng + at) * rows, rows)
                outs[k][0, i] = half(total[pl.ds(start, rows), :columns])
        for k in range(ny):
            at = lax.rem(y + k, ny)
            for i in range(ng):
                start = pl.multiple_of((at * ng + i) * rows, rows)
                outs[ng + k][0, i] = half(total[pl.ds(start, rows), columns:])

    first = jax.ShapeDtypeStruct((nz, ny, rows, columns), BF)
    second = jax.ShapeDtypeStruct((nz, ng, rows, columns), BF)
    step = height // nz
    skip = (more[0].shape[0] - height) // step if more else 0
    outs = pl.pallas_call(
        kernel,
        grid=(nz,),
        in_specs=[whole(pltpu.SMEM)]
        + [pl.BlockSpec((tokens, step), lambda i: (0, i))] * n
        + [pl.BlockSpec((n * tokens, right_width), lambda i: (0, 0))]
        + [pl.BlockSpec((step, v.shape[1]), lambda i: (i + skip, 0)) for v in more],
        out_specs=[pl.BlockSpec((1, ny, rows, columns), lambda i: (i, 0, 0, 0))] * ng
        + [pl.BlockSpec((1, ng, rows, columns), lambda i: (i, 0, 0, 0))] * ny,
        out_shape=[first] * ng + [second] * ny,
        scratch_shapes=[pltpu.VMEM((step, width), F32)],
        compiler_params=pltpu.CompilerParams(vmem_limit_bytes=20 << 20),
        cost_estimate=cost(7),
        name="weight_grad",
    )(place, *left, right, *more)
    return outs[:ng], outs[ng:]


def total_of(refs, at):
    value = refs[0][at].astype(F32)
    for ref in refs[1:]:
        value = value + ref[at].astype(F32)
    return value


def add_split(place, sizes, first, second):
    nz, ny, ng = sizes
    rows, columns = first[0].shape[2:]

    def kernel(place_ref, *refs):
        firsts, seconds, outs = refs[:ng], refs[ng : ng + ny], refs[ng + ny :]
        y, g = place_ref[1], place_ref[2]
        for k in range(ny):
            outs[k][0] = half(total_of(firsts, (0, lax.rem(y + k, ny))))
        for k in range(ng):
            outs[ny + k][0] = half(total_of(seconds, (0, lax.rem(g + k, ng))))

    shape = jax.ShapeDtypeStruct((nz, rows, columns), BF)
    outs = pl.pallas_call(
        kernel,
        grid=(nz,),
        in_specs=[whole(pltpu.SMEM)]
        + [pl.BlockSpec((1, ny, rows, columns), lambda i: (i, 0, 0, 0))] * ng
        + [pl.BlockSpec((1, ng, rows, columns), lambda i: (i, 0, 0, 0))] * ny,
        out_specs=[pl.BlockSpec((1, rows, columns), lambda i: (i, 0, 0))] * (ny + ng),
        out_shape=[shape] * (ny + ng),
        compiler_params=pltpu.CompilerParams(vmem_limit_bytes=12 << 20),
        cost_estimate=cost(3.5),
        name="add_split",
    )(place, *[*first, *second])
    return outs[:ny], outs[ny:]


def split_over_z(first, second, more):
    ny, ng = len(first), len(second)
    nz, rows, columns = first[0].shape
    extra = [] if more is None else [more]
    count = 0 if more is None else more.shape[1]
    n_in = ny + ng + len(extra)

    def kernel(*refs):
        out = refs[n_in]
        out[0, :rows, :columns] = half(total_of(refs[:ny], 0))
        out[0, :rows, columns:] = half(total_of(refs[ny : ny + ng], 0))
        if extra:
            out[0, rows:] = half(refs[n_in - 1][0])

    return pl.pallas_call(
        kernel,
        grid=(nz,),
        in_specs=[pl.BlockSpec((1, rows, columns), lambda i: (i, 0, 0))] * (ny + ng)
        + [pl.BlockSpec((1, *m.shape[1:]), lambda i: (i, 0, 0)) for m in extra],
        out_specs=pl.BlockSpec((1, rows + count, 2 * columns), lambda i: (i, 0, 0)),
        out_shape=jax.ShapeDtypeStruct((nz, rows + count, 2 * columns), BF),
        compiler_params=pltpu.CompilerParams(vmem_limit_bytes=12 << 20),
        cost_estimate=cost(2.5),
        name="split_over_z",
    )(*first, *second, *extra)


def split_both_over_z(first, second, third, fourth):
    ny, ng = len(first), len(second)
    nz, rows, columns = first[0].shape
    high, low_columns = third[0].shape[1:]
    groups = high // rows

    def kernel(*refs):
        parts = (refs[:ny], refs[ny : ny + ng], refs[ny + ng : 2 * ny + ng], refs[2 * ny + ng : -1])
        out = refs[-1]
        for i in range(2):
            out[0, :rows, i * columns : (i + 1) * columns] = half(total_of(parts[i], 0))
            total = half(total_of(parts[2 + i], 0))
            for j in range(groups):
                start = (2 * j + i) * low_columns
                out[0, rows:, start : start + low_columns] = total[j * rows : (j + 1) * rows]

    return pl.pallas_call(
        kernel,
        grid=(nz,),
        in_specs=[pl.BlockSpec((1, rows, columns), lambda i: (i, 0, 0))] * (ny + ng)
        + [pl.BlockSpec((1, high, low_columns), lambda i: (i, 0, 0))] * (ny + ng),
        out_specs=pl.BlockSpec((1, 2 * rows, 2 * columns), lambda i: (i, 0, 0)),
        out_shape=jax.ShapeDtypeStruct((nz, 2 * rows, 2 * columns), BF),
        compiler_params=pltpu.CompilerParams(vmem_limit_bytes=12 << 20),
        cost_estimate=cost(3),
        name="split_both_over_z",
    )(*first, *second, *third, *fourth)


def send_parts(first, second, axis_first, axis_second):
    first = [first[0]] + [shift(b, axis_first, k) for k, b in enumerate(first) if k]
    second = [second[0]] + [shift(b, axis_second, k) for k, b in enumerate(second) if k]
    return first, second


def reduce_in_layer(place, sizes, parts, *others):
    first, second = parts
    first = [after(first[0], *others)] + first[1:]
    return send_parts(*add_split(place, sizes, first, second), "y", "g")


def over_z(blocks):
    return lax.all_to_all(blocks, "z", 0, 0, tiled=True)


def total_sum(blocks):
    total = blocks[0].astype(F32)
    for block in blocks[1:]:
        total = total + block.astype(F32)
    return total


def key_blocks(start, block):
    return range(max(0, start - DOC_MAX), start + block, block)


def visible_part(first_ref, low, start, block, rows, row):
    key_pos = low + row + lax.broadcasted_iota(jnp.int32, (rows, block), 0)
    visible = key_pos >= first_ref[:, start : start + block]
    if low == start:
        visible &= key_pos <= start + lax.broadcasted_iota(jnp.int32, (rows, block), 1)
    return visible


def fold(values, op):
    rows, lanes = values.shape
    return op(values.reshape(rows // 8, 8, lanes), axis=0)


def for_heads(values, head_dim):
    lane = lax.broadcasted_iota(jnp.int32, values.shape, 1) // head_dim
    heads = values.shape[1] // head_dim
    return jnp.concatenate([jnp.where(lane == h, values, jnp.zeros_like(values)) for h in range(heads)], axis=0)


def heads_of(values, head_dim, block):
    heads = values.shape[0] // head_dim
    return jnp.concatenate(
        [values[h * head_dim : (h + 1) * head_dim, h * block : (h + 1) * block] for h in range(heads)], axis=0
    )


def load_in_order(order_ref, source, into, local, columns):
    for n in range(into.shape[0] // local):
        rows = pl.ds(pl.multiple_of(order_ref[n] * local, local), local)
        into[n * local : (n + 1) * local] = source[rows, columns]


def store_in_order(order_ref, source, into, local, columns):
    for n in range(source.shape[0] // local):
        rows = pl.ds(pl.multiple_of(order_ref[n] * local, local), local)
        into[rows, columns] = half(source[n * local : (n + 1) * local])


def attend_kernel(block, sub, head_dim, local, order_ref, qkv_ref, first_ref, out_ref, log_ref, q_s, k_s, v_s, o_s, s_s):
    length, lanes = q_s.shape
    heads = lanes // head_dim
    for i, into in enumerate((q_s, k_s, v_s)):
        load_in_order(order_ref, qkv_ref, into, local, slice(i * lanes, (i + 1) * lanes))
    v_t = v_s[...].T
    for start in range(0, length, block):
        q_heads = for_heads(q_s[start : start + block] * (head_dim ** (-0.5)), head_dim)
        lows = list(key_blocks(start, block))
        top8 = [jnp.full((8, block), -1e30, F32)] * heads
        for n, low in enumerate(lows):
            scores = dot(k_s[low : low + block], q_heads, (1, 1))
            for r in range(0, block, sub):
                visible = visible_part(first_ref, low, start, block, sub, r)
                rows = slice(n * block + r, n * block + r + sub)
                for h in range(heads):
                    columns = slice(h * block, (h + 1) * block)
                    piece = jnp.where(visible, scores[r : r + sub, columns], -1e30)
                    top8[h] = jnp.maximum(top8[h], fold(piece, jnp.max))
                    s_s[rows, columns] = piece
        width = len(lows) * block
        top = jnp.concatenate([jnp.max(v, axis=0, keepdims=True) for v in top8], axis=1)
        total8 = jnp.zeros((8, heads * block), F32)
        for r in range(0, width, sub):
            exponent = jnp.exp(s_s[r : r + sub] - top)
            total8 = total8 + fold(exponent, jnp.sum)
            s_s[r : r + sub] = exponent
        total = jnp.sum(total8, axis=0, keepdims=True)
        probs = half(s_s[:width] * (1.0 / total))
        out = dot(v_t[:, lows[0] : lows[0] + width], probs, (1, 0))
        log = top + jnp.log(total)
        for h in range(heads):
            log_ref[0, h : h + 1, start : start + block] = log[:, h * block : (h + 1) * block]
        o_s[start : start + block] = half(heads_of(out, head_dim, block).T)
    store_in_order(order_ref, o_s, out_ref, local, slice(None))


def attend_back_kernel(
    block,
    sub,
    head_dim,
    local,
    order_ref,
    qkv_ref,
    g_refs,
    log_ref,
    first_ref,
    out_ref,
    sum_ref,
    q_s,
    k_s,
    v_s,
    g_s,
    g_raw,
    query_grad,
    key_sum,
    value_sum,
    p_s,
    d_s,
):
    length, lanes = q_s.shape
    heads = lanes // head_dim
    scale = head_dim ** (-0.5)
    for i, into in enumerate((q_s, k_s, v_s)):
        load_in_order(order_ref, qkv_ref, into, local, slice(i * lanes, (i + 1) * lanes))
    own = g_refs[0].shape[0]
    for i, ref in enumerate(g_refs):
        g_raw[i * own : (i + 1) * own] = ref[...]
    load_in_order(order_ref, g_raw, g_s, local, slice(None))
    k_t = k_s[...].T
    for start in range(0, length, block):
        q_heads = for_heads(q_s[start : start + block] * scale, head_dim)
        g_heads = for_heads(g_s[start : start + block], head_dim)
        lows = list(key_blocks(start, block))
        delta8 = [jnp.zeros((8, block), F32)] * heads
        for n, low in enumerate(lows):
            scores = dot(k_s[low : low + block], q_heads, (1, 1))
            grads = dot(v_s[low : low + block], g_heads, (1, 1))
            for r in range(0, block, sub):
                visible = visible_part(first_ref, low, start, block, sub, r)
                rows = slice(n * block + r, n * block + r + sub)
                for h in range(heads):
                    columns = slice(h * block, (h + 1) * block)
                    p = jnp.where(visible, scores[r : r + sub, columns], -1e30)
                    p = jnp.exp(p - log_ref[0, h : h + 1, start : start + block])
                    d = grads[r : r + sub, columns]
                    delta8[h] = delta8[h] + fold(p * d, jnp.sum)
                    p_s[rows, columns] = p
                    d_s[rows, columns] = d
        delta = jnp.concatenate([jnp.sum(v, axis=0, keepdims=True) for v in delta8], axis=1)
        width = len(lows) * block
        p = p_s[:width]
        grad_scores = half(p * (d_s[:width] - delta))
        dq = dot(k_t[:, lows[0] : lows[0] + width], grad_scores, (1, 0))
        dk = dot(grad_scores, q_heads, (1, 0))
        dv = dot(half(p), g_heads, (1, 0))
        for n, low in enumerate(lows):
            rows = slice(n * block, (n + 1) * block)
            if low == start:
                key_sum[low : low + block] = dk[rows]
                value_sum[low : low + block] = dv[rows]
            else:
                key_sum[low : low + block] += dk[rows]
                value_sum[low : low + block] += dv[rows]
        query_grad[start : start + block] = (heads_of(dq, head_dim, block) * scale).T
    for i, source in enumerate((query_grad, key_sum, value_sum)):
        columns = slice(i * lanes, (i + 1) * lanes)
        store_in_order(order_ref, source, out_ref, local, columns)
        sum_ref[:, columns] = jnp.sum(half(source[...]).astype(F32), axis=0, keepdims=True)


def attend(qkv, first, order, local, head_dim):
    length, width = qkv.shape
    block = min(256, length)
    window = min(length, DOC_MAX + block)
    lanes = 2 * head_dim
    steps = width // (3 * lanes)

    def kernel(*refs):
        attend_kernel(block, 64, head_dim, local, *refs)

    return pl.pallas_call(
        kernel,
        grid=(steps,),
        in_specs=[
            whole(pltpu.SMEM),
            pl.BlockSpec((length, 3 * lanes), lambda i: (0, i)),
            pl.BlockSpec((1, length), lambda i: (0, 0)),
        ],
        out_specs=[
            pl.BlockSpec((length, lanes), lambda i: (0, i)),
            pl.BlockSpec((1, 2, length), lambda i: (i, 0, 0)),
        ],
        out_shape=[
            jax.ShapeDtypeStruct((length, width // 3), BF),
            jax.ShapeDtypeStruct((steps, 2, length), F32),
        ],
        scratch_shapes=[pltpu.VMEM((length, lanes), BF)] * 4 + [pltpu.VMEM((window, 2 * block), F32)],
        compiler_params=pltpu.CompilerParams(vmem_limit_bytes=16 << 20),
        cost_estimate=cost(11.5 * steps / 4),
        name="attend",
    )(order, qkv, first[None])


def attend_back(qkv, grad_out, logs, first, order, local, head_dim):
    length, width = qkv.shape
    block = min(256, length)
    window = min(length, DOC_MAX + block)
    lanes = 2 * head_dim
    steps = width // (3 * lanes)

    n = len(grad_out)
    own = length // n

    def kernel(order_ref, qkv_ref, *refs):
        attend_back_kernel(block, 64, head_dim, local, order_ref, qkv_ref, refs[:n], *refs[n:])

    return pl.pallas_call(
        kernel,
        grid=(steps,),
        in_specs=[
            whole(pltpu.SMEM),
            pl.BlockSpec((length, 3 * lanes), lambda i: (0, i)),
        ]
        + [pl.BlockSpec((own, lanes), lambda i: (0, i))] * n
        + [
            pl.BlockSpec((1, 2, length), lambda i: (i, 0, 0)),
            pl.BlockSpec((1, length), lambda i: (0, 0)),
        ],
        out_specs=[
            pl.BlockSpec((length, 3 * lanes), lambda i: (0, i)),
            pl.BlockSpec((1, 3 * lanes), lambda i: (0, i)),
        ],
        out_shape=[jax.ShapeDtypeStruct((length, width), BF), jax.ShapeDtypeStruct((1, width), F32)],
        scratch_shapes=[pltpu.VMEM((length, lanes), BF)] * 5
        + [pltpu.VMEM((length, lanes), F32)] * 3
        + [pltpu.VMEM((window, 2 * block), F32)] * 2,
        compiler_params=pltpu.CompilerParams(vmem_limit_bytes=20 << 20),
        cost_estimate=cost(18 * steps / 4),
        name="attend_back",
    )(order, qkv, *grad_out, logs, first[None])


def product(left, right, contract, kind, bias=None, rows=None, part=0):
    rows = left.shape[0] if rows is None else rows
    depth = left.shape[1]
    width = right.shape[1 - contract[1]]
    block = min(256, width)
    extra = [] if bias is None else [bias[None]]

    def kernel(left_ref, right_ref, *refs):
        out = dot(left_ref[...], right_ref[...], contract)
        if extra:
            out = out + refs[0][...]
        refs[-1][...] = out.astype(kind)

    if contract[1] == 0:
        right_spec = pl.BlockSpec((depth, block), lambda i: (0, i))
    else:
        right_spec = pl.BlockSpec((block, depth), lambda i: (i, 0))
    return pl.pallas_call(
        kernel,
        grid=(width // block,),
        in_specs=[pl.BlockSpec((rows, depth), lambda i: (part, 0)), right_spec]
        + [pl.BlockSpec((1, block), lambda i: (0, i)) for _ in extra],
        out_specs=pl.BlockSpec((rows, block), lambda i: (0, i)),
        out_shape=jax.ShapeDtypeStruct((rows, width), kind),
        compiler_params=pltpu.CompilerParams(vmem_limit_bytes=16 << 20),
        cost_estimate=cost(2.3 * rows * width * depth / 2**30),
        name="product",
    )(*(pltpu.with_memory_space_constraint(a, pltpu.HBM) for a in (left, right)), *extra)


def norm_back_part(summands, values, gain, added, scale=None):
    tokens, width = values.shape
    block = min(128, tokens)
    n = len(summands)

    def kernel(*refs):
        ins, outs = refs[: n + 3], refs[n + 3 :]

        @pl.when(pl.program_id(0) == 0)
        def _():
            for ref in outs[1 if scale is None else 2 :]:
                ref[...] = jnp.zeros_like(ref)

        grad = ins[0][...].astype(F32)
        for ref in ins[1:n]:
            grad = grad + ref[...].astype(F32)
        normal, inverse = norm_parts(ins[n][...].astype(F32))
        out = ins[n + 2][...].astype(F32) + norm_back(grad, normal, inverse, ins[n + 1][...])
        sums = [grad * normal, grad]
        if scale is None:
            outs[0][...] = half(out)
            rest = outs[1:]
        else:
            outs[0][...] = out
            scaled = half(scale * out)
            outs[1][...] = scaled
            sums.append(scaled.astype(F32))
            rest = outs[2:]
        for ref, value in zip(rest, sums):
            ref[...] += jnp.sum(value, axis=0, keepdims=True)

    row = pl.BlockSpec((block, width), lambda i: (i, 0))
    one = pl.BlockSpec((1, width), lambda i: (0, 0))
    total = jax.ShapeDtypeStruct((1, width), F32)
    if scale is None:
        out_specs, out_shape = [row, one, one], [jax.ShapeDtypeStruct((tokens, width), BF), total, total]
    else:
        out_specs = [row, row, one, one, one]
        out_shape = [
            jax.ShapeDtypeStruct((tokens, width), F32),
            jax.ShapeDtypeStruct((tokens, width), BF),
            total,
            total,
            total,
        ]
    return pl.pallas_call(
        kernel,
        grid=(tokens // block,),
        in_specs=[row] * n + [row, one, row],
        out_specs=out_specs,
        out_shape=out_shape,
        compiler_params=pltpu.CompilerParams(vmem_limit_bytes=16 << 20),
        cost_estimate=cost(3),
        name="norm_back_part",
    )(*summands, values, gain[None], added)


def proj_norm(here, parts, weights, bias, gain, shift_by, x, depth):
    nt = len(parts)
    tokens, width = x.shape
    part = width // nt
    block = min(128, tokens)

    def kernel(here_ref, *refs):
        parts_in, weights_in = refs[:nt], refs[nt : 2 * nt]
        bias_ref, gain_ref, shift_ref, x_ref, hidden_ref, normed_ref = refs[2 * nt :]
        t = here_ref[0]
        for j in range(nt):
            total = 0.0
            for k in range(nt):
                rows = pl.ds(pl.multiple_of(lax.rem(t + k, nt) * part, part), part)
                total = total + dot(parts_in[k][...], weights_in[j][rows, :], (1, 0))
            columns = pl.ds(pl.multiple_of(lax.rem(t - j + nt, nt) * part, part), part)
            hidden_ref[:, columns] = x_ref[:, columns].astype(F32) + depth * (total + bias_ref[:, columns])
        normal, _ = norm_parts(hidden_ref[...])
        normed_ref[...] = half(normal * gain_ref[...] + shift_ref[...])

    row = pl.BlockSpec((block, width), lambda i: (i, 0))
    one = pl.BlockSpec((1, width), lambda i: (0, 0))
    return pl.pallas_call(
        kernel,
        grid=(tokens // block,),
        in_specs=[whole(pltpu.SMEM)]
        + [pl.BlockSpec((block, part), lambda i: (i, 0))] * nt
        + [pl.BlockSpec((width, part), lambda i: (0, 0))] * nt
        + [one, one, one, row],
        out_specs=[row, row],
        out_shape=[jax.ShapeDtypeStruct((tokens, width), F32), jax.ShapeDtypeStruct((tokens, width), BF)],
        compiler_params=pltpu.CompilerParams(vmem_limit_bytes=16 << 20),
        cost_estimate=cost(3),
        name="proj_norm",
    )(here, *parts, *weights, bias[None], gain[None], shift_by[None], x)


def proj_back(here, grad, parts, weights):
    nt = len(parts)
    tokens, width = grad.shape
    part = width // nt

    def kernel(here_ref, grad_ref, *refs):
        parts_in, weights_in, outs = refs[:nt], refs[nt : 2 * nt], refs[2 * nt :]
        t = here_ref[0]

        def place(step, offset=0):
            return pl.ds(pl.multiple_of(lax.rem(t + step + nt, nt) * part + offset, 128), part)

        for k in range(nt):
            total = 0.0
            for j in range(nt):
                total = total + dot(grad_ref[:, place(-j)], weights_in[j][place(k), :], (1, 1))
            outs[k][:tokens] = half(total)
        for k in range(nt):
            for m in range(nt):
                outs[k][place(m, tokens), :] = half(dot(parts_in[m][...], grad_ref[:, place(k)], (0, 0)))

    return pl.pallas_call(
        kernel,
        in_specs=[whole(pltpu.SMEM)] + [whole()] * (1 + 2 * nt),
        out_specs=[whole()] * nt,
        out_shape=[jax.ShapeDtypeStruct((tokens + width, part), BF)] * nt,
        compiler_params=pltpu.CompilerParams(vmem_limit_bytes=24 << 20),
        cost_estimate=cost(4),
        name="proj_back",
    )(here, grad, *parts, *weights)


def gelu_parts(u):
    c = 0.7978845608028654
    square = u * u
    h = 0.5 + 0.5 * jnp.tanh(u * (c + (c * 0.044715) * square))
    value = u * h
    return value, h + value * (1.0 - h) * (2 * c + (6 * c * 0.044715) * square)


def up_part(normed, weight, bias):
    n = len(normed)
    tokens, width = normed[0].shape
    ff = weight.shape[1]
    block = min(256, ff)
    rows = min(512, tokens)

    def kernel(*refs):
        w_ref, b_ref, active_ref, slope_ref = refs[n:]
        for i in range(n):
            for r in range(0, tokens, rows):
                u = dot(refs[i][r : r + rows], w_ref[...], (1, 0)) + b_ref[...]
                value, slope = gelu_parts(u)
                at = slice(i * tokens + r, i * tokens + r + rows)
                active_ref[at] = half(value)
                slope_ref[at] = half(slope)

    column = pl.BlockSpec((n * tokens, block), lambda i: (0, i))
    return pl.pallas_call(
        kernel,
        grid=(ff // block,),
        in_specs=[pl.BlockSpec((tokens, width), lambda i: (0, 0))] * n
        + [
            pl.BlockSpec((width, block), lambda i: (0, i)),
            pl.BlockSpec((1, block), lambda i: (0, i)),
        ],
        out_specs=[column, column],
        out_shape=[jax.ShapeDtypeStruct((n * tokens, ff), BF)] * 2,
        compiler_params=pltpu.CompilerParams(vmem_limit_bytes=16 << 20),
        cost_estimate=cost(7),
        name="up_part",
    )(*normed, weight, bias[None])


def up_back(grad_down, weight, slope):
    tokens, width = grad_down.shape
    ff = weight.shape[0]
    block = min(256, ff)
    rows = min(512, tokens)

    def kernel(g_ref, w_ref, slope_ref, out_ref, sum_ref):
        total = jnp.zeros((8, block), F32)
        for r in range(0, tokens, rows):
            grad = half(dot(g_ref[r : r + rows], w_ref[...], (1, 1)) * slope_ref[r : r + rows])
            out_ref[r : r + rows] = grad
            total = total + fold(grad.astype(F32), jnp.sum)
        sum_ref[...] = jnp.sum(total, axis=0, keepdims=True)

    column = pl.BlockSpec((tokens, block), lambda i: (0, i))
    return pl.pallas_call(
        kernel,
        grid=(ff // block,),
        in_specs=[
            pl.BlockSpec((tokens, width), lambda i: (0, 0)),
            pl.BlockSpec((block, width), lambda i: (i, 0)),
            column,
        ],
        out_specs=[column, pl.BlockSpec((1, block), lambda i: (0, i))],
        out_shape=[jax.ShapeDtypeStruct((tokens, ff), BF), jax.ShapeDtypeStruct((1, ff), F32)],
        compiler_params=pltpu.CompilerParams(vmem_limit_bytes=16 << 20),
        cost_estimate=cost(6.5),
        name="up_back",
    )(*[grad_down, weight, slope])


def body(
    block_input,
    doc_ids,
    gain_attn,
    shift_attn,
    w_qkv,
    bias_qv,
    w_proj,
    bias_proj,
    gain_mlp,
    shift_mlp,
    w_up,
    bias_up,
    w_down,
    bias_down,
    out_grad,
):
    nz, ny, ng, nt = (lax.axis_size(a) for a in ("z", "y", "g", "t"))
    sizes = (nz, ny, ng)
    z, y, g, t = (lax.axis_index(a) for a in ("z", "y", "g", "t"))
    place = jnp.stack([z, y, g]).astype(jnp.int32)
    chips = nz * ny * ng
    depth = LAYERS ** (-0.5)
    _, local, width = block_input.shape
    length = doc_ids.shape[1]
    shard = w_qkv.shape[0]
    part = width // nt
    head_dim = width // H
    lanes = 2 * head_dim
    pairs = part // lanes
    hidden_width = w_up.shape[1]
    ff_shard = w_down.shape[0]
    ff_part = hidden_width // nt
    own = ng * local
    block_rows = nt * shard

    natural = jnp.arange(ng * nt, dtype=jnp.int32)
    order = lax.rem(t - natural % nt + nt, nt) * ng + lax.rem(g - natural // nt + ng, ng)
    docs = lax.dynamic_index_in_dim(doc_ids, g, 0, keepdims=False)
    first_token = jnp.sum((docs[None, :] < docs[:, None]).astype(jnp.int32), axis=1)

    both = jnp.stack([block_input, out_grad], axis=1)
    parts = []
    for k in range(ng):
        block = lax.dynamic_index_in_dim(both, lax.rem(g + k, ng), 0, keepdims=False)
        parts.append(shift(block, "g", k) if k else block)
    both_own = jnp.concatenate(parts, axis=1)
    x_own, grad_own = both_own[0], both_own[1]
    both_all = jnp.concatenate(gather_relative(both_own, "t"), axis=1)

    vectors = [gain_attn, shift_attn, bias_qv, bias_proj, gain_mlp, shift_mlp, bias_up, bias_down]
    counts = [v.shape[0] for v in vectors]
    packed = half(lax.optimization_barrier(jnp.concatenate(vectors)))
    count = packed.shape[0]
    columns_a = half(w_qkv).reshape(shard, 3, nt, pairs, lanes).transpose(2, 0, 3, 1, 4).reshape(nt, shard, 3 * part)
    columns_o = half(w_proj).reshape(shard, nt, part).transpose(1, 0, 2)
    columns_u = half(w_up).reshape(shard, chips, nt, ff_shard).transpose(2, 0, 1, 3).reshape(nt, shard, ff_part)
    columns = jnp.concatenate([columns_a, columns_o, columns_u], axis=2)
    wide = columns.shape[2]
    packed = jnp.broadcast_to(jnp.pad(packed, (0, wide - count)), (nt, 8, wide))
    columns = swap_axis(jnp.concatenate([columns, packed], axis=1), "t", 0)
    packed = jnp.concatenate([c[shard : shard + 1, :count] for c in columns], axis=1)
    columns = jnp.concatenate([c[:shard] for c in columns], axis=0)
    packed = jnp.broadcast_to(jnp.pad(packed, ((0, 0), (0, 4 * part - nt * count))), (8, 4 * part))
    shard_a = jnp.concatenate([columns[:, : 4 * part], packed], axis=0)
    shard_u = columns[:, 4 * part :]
    shard_d = half(w_down)
    middle_d = width // 2

    first_d, second_d = gather_once(shard_d[:, :middle_d], shard_d[:, middle_d:])
    first_a, second_a = halves(gather_over_z(after(shard_a, first_d, second_d)))
    first_u, second_u = halves(gather_over_z(after(shard_u, first_a, second_a)))
    first_a, second_a = gather_once(first_a, second_a)
    both_d = jnp.concatenate([first_d, second_d], axis=0)
    both_d = gather_over_z(after(both_d, first_u, second_u, first_a, second_a))
    first_a, second_a = gather_twice(first_a, second_a)
    side = 3 * part - 2 * part
    wqkv, wo, vector_rows = assemble(
        place,
        first_a,
        second_a,
        [
            [(0, 0, block_rows, 0, 2 * part, 0), (1, 0, block_rows, 0, side, 2 * part)],
            [(1, 0, block_rows, side, part, 0)],
            [(0, block_rows, 8, 0, 2 * part, 0)],
        ],
        [(block_rows, 3 * part), (block_rows, part), (8, 2 * part)],
    )
    wqkv = wqkv.reshape(width, 3 * part)
    wo = wo.reshape(width, part)
    first_u, second_u = gather_once(after(first_u, *first_a, *second_a), after(second_u, *first_a, *second_a))

    vector_rows = vector_rows.reshape(chips, 8, 2 * part)[:, 0, : nt * count].reshape(chips, nt, count)
    offsets = [0]
    for size in counts:
        offsets.append(offsets[-1] + size)
    pieces = [vector_rows[:, :, offsets[i] : offsets[i + 1]] for i in range(len(counts))]
    h_gain_attn, h_shift_attn, h_bias_qv, h_bias_proj, h_gain_mlp, h_shift_mlp = (
        p.reshape(-1).astype(F32) for p in pieces[:6]
    )
    h_bias_down = pieces[7].reshape(-1).astype(F32)
    h_bias_up = lax.dynamic_index_in_dim(pieces[6], t, 1, keepdims=False).astype(F32).reshape(-1)
    bias_q = lax.dynamic_slice_in_dim(h_bias_qv, t * part, part).reshape(pairs, lanes)
    bias_v = lax.dynamic_slice_in_dim(h_bias_qv, width + t * part, part).reshape(pairs, lanes)
    bias_qkv = jnp.stack([bias_q, jnp.zeros_like(bias_q), bias_v], axis=1).reshape(-1)

    normal_all, _ = norm_parts(both_all[0].astype(F32))
    normed_attn = half(normal_all * h_gain_attn + h_shift_attn)
    grad_down = half(depth * both_all[1].astype(F32))
    d_bias_down = jnp.sum(grad_down[:own], axis=0, dtype=F32)
    normed_attn = after(normed_attn, d_bias_down)
    qkv = product(normed_attn, wqkv, (1, 0), BF, bias_qkv)
    qkv = after(qkv, first_u, second_u)
    attended_heads, logs = attend(qkv, first_token, order, local, head_dim)
    first_u, second_u = gather_twice(first_u, second_u)
    wo_parts = gather_relative(wo, "t")
    attended_parts = return_relative([attended_heads[k * own : (k + 1) * own] for k in range(nt)], "t")
    here = t.astype(jnp.int32)[None]
    hidden, normed_own = proj_norm(
        here,
        attended_parts,
        wo_parts,
        h_bias_proj,
        h_gain_mlp,
        h_shift_mlp,
        after(x_own, *first_u, *second_u),
        depth,
    )
    normed_mlp = gather_relative(normed_own, "t")
    (wu,) = assemble(
        place,
        first_u,
        second_u,
        [[(0, 0, block_rows, 0, ff_part // 2, 0), (1, 0, block_rows, 0, ff_part // 2, ff_part // 2)]],
        [(block_rows, ff_part)],
    )
    wu = wu.reshape(width, ff_part)
    first_d, second_d = both_d[:, :ng].swapaxes(0, 1), both_d[:, ng:].swapaxes(0, 1)
    first_d, second_d = gather_twice(after(first_d, *first_u, *second_u), after(second_d, *first_u, *second_u))
    active, slope = up_part(normed_mlp, wu, h_bias_up)

    def own_sum(left, right, contract):
        blocks = [product(left, right, contract, BF, rows=own, part=k) for k in range(1, nt)]
        mine = product(after(left, *blocks), right, contract, F32, rows=own)
        return [mine] + [shift(block, "t", -k - 1) for k, block in enumerate(blocks)]

    down_blocks = weight_grad(place, sizes, [active], grad_down)
    down_parts = send_parts(*down_blocks, "g", "y")
    (wd,) = assemble(
        place,
        first_d,
        second_d,
        [[(0, 0, ff_shard, 0, middle_d, 0), (1, 0, ff_shard, 0, middle_d, middle_d)]],
        [(ff_shard, width)],
    )
    wd = wd.reshape(ff_part, width)
    grad_up, d_bias_up = up_back(after(grad_down, *down_blocks[0]), wd, slope)
    up_blocks = weight_grad(place, sizes, normed_mlp, grad_up)
    down_parts = reduce_in_layer(place, sizes, down_parts, *up_blocks[0])
    up_parts = send_parts(*up_blocks, "g", "y")
    e2 = own_sum(after(grad_up, up_blocks[0][0]), wu, (1, 1))

    grad_hidden, grad_branch, d_gain_mlp, d_shift_mlp, d_bias_proj = norm_back_part(
        e2, after(hidden, down_parts[0][0]), h_gain_mlp, grad_own, depth
    )


    def to_rows(blocks):
        return jnp.stack(by_place(return_relative([blocks[k] for k in range(ng)], "g"), "g", 1), axis=0)

    lowered = own_sum(after(active, grad_branch), wd, (1, 0))
    up_parts = reduce_in_layer(place, sizes, up_parts, lowered[0])
    back_parts = proj_back(here, after(grad_branch, up_parts[0][0]), attended_parts, wo_parts)
    back_parts = [back_parts[0]] + [shift(b, "t", k) for k, b in enumerate(back_parts) if k]
    block_out = half(hidden + depth * (total_sum(lowered) + h_bias_down)).reshape(ng, local, width)
    grad_attended = [after(b, block_out) for b in back_parts]

    def to_rows(blocks):
        return jnp.stack(by_place(return_relative([blocks[k] for k in range(ng)], "g"), "g", 1), axis=0)

    d_qkv, d_bias_qkv = attend_back(qkv, grad_attended, logs, first_token, order, local, head_dim)
    a_blocks = weight_grad(place, sizes, [normed_attn], d_qkv, back_parts)
    a_parts = send_parts(*a_blocks, "g", "y")
    d_qkv = after(d_qkv, *a_blocks[0])
    both_split = split_both_over_z([after(up_parts[0][0], d_qkv)] + up_parts[0][1:], up_parts[1], *down_parts)
    both_sent = over_z(both_split)
    d_qkv = after(d_qkv, both_split)
    e1 = own_sum(d_qkv, wqkv, (1, 1))
    grad_input, d_gain_attn, d_shift_attn = norm_back_part(e1, x_own, h_gain_attn, grad_hidden)
    def by_owner(full):
        return full.reshape(chips, nt, -1)

    d_bias_qkv = d_bias_qkv.reshape(pairs, 3, lanes)
    d_bias_qv = jnp.zeros((2 * width,), F32)
    d_bias_qv = lax.dynamic_update_slice_in_dim(d_bias_qv, d_bias_qkv[:, 0].reshape(-1), t * part, 0)
    d_bias_qv = lax.dynamic_update_slice_in_dim(d_bias_qv, d_bias_qkv[:, 2].reshape(-1), width + t * part, 0)
    d_bias_up = d_bias_up.reshape(chips, 1, ff_shard)
    d_bias_up = jnp.where(lax.broadcasted_iota(jnp.int32, (chips, nt, 1), 1) == t, d_bias_up, 0.0)
    sums = jnp.concatenate(
        [
            by_owner(d_gain_attn),
            by_owner(d_shift_attn),
            by_owner(d_bias_qv),
            by_owner(d_bias_proj),
            by_owner(d_gain_mlp),
            by_owner(d_shift_mlp),
            d_bias_up,
            by_owner(d_bias_down),
        ],
        axis=2,
    )
    sums = sums.reshape(nz, ny * ng, nt * count)
    a_parts = reduce_in_layer(place, sizes, a_parts, sums)
    sums = reduce_axes(sums, ("y", "g"), 1)
    high = half(sums)
    more = jnp.stack([high.astype(F32), sums - high.astype(F32)], axis=1)
    more = jnp.pad(more, ((0, 0), (0, 6), (0, 4 * part - nt * count)))
    a_blocks = split_over_z(*a_parts, after(more, both_sent))
    block_out = to_rows(after(block_out, a_blocks))
    grad_input = to_rows(after(grad_input, a_blocks).reshape(ng, local, width)).astype(F32)
    both = jnp.sum(after(both_sent, a_blocks).astype(F32), axis=0)
    sum_up = both[:block_rows]
    sum_down = jnp.concatenate(jnp.split(both[block_rows:], ff_part // width, axis=1), axis=0)
    sum_a = jnp.sum(over_z(a_blocks).astype(F32), axis=0)
    sums = (sum_a[block_rows, : nt * count] + sum_a[block_rows + 1, : nt * count]).reshape(nt, 1, count)
    sums = jnp.pad(sums, ((0, 0), (0, 7), (0, 4 * part - count)))
    rest = jnp.concatenate([sum_a[:block_rows].reshape(nt, shard, 4 * part), sums], axis=1)
    rest = swap_axis(rest, "t", 0)
    sums = total_sum([r[shard, :count] for r in rest])
    rest = [r[:shard] for r in rest]
    out_vectors = [sums[offsets[i] : offsets[i + 1]] for i in range(len(counts))]

    up = swap_axis(sum_up.reshape(nt, shard, ff_part), "t", 0)
    sum_up = jnp.stack([u.reshape(shard, chips, ff_shard) for u in up], axis=2).reshape(shard, hidden_width)
    sum_qkv = jnp.stack([r[:, : 3 * part].reshape(shard, pairs, 3, lanes) for r in rest], axis=1)
    sum_qkv = sum_qkv.transpose(0, 3, 1, 2, 4).reshape(shard, 3 * width)
    sum_proj = jnp.concatenate([r[:, 3 * part :] for r in rest], axis=1)
    return (
        block_out,
        grad_input,
        out_vectors[0],
        out_vectors[1],
        sum_qkv,
        out_vectors[2],
        sum_proj,
        out_vectors[3],
        out_vectors[4],
        out_vectors[5],
        sum_up,
        out_vectors[6],
        sum_down,
        out_vectors[7],
    )


def solution(mesh):
    rows = 2
    dp, seq = mesh.shape["dp"], mesh.shape["seq"]
    high = 4
    split = Mesh(mesh.devices.reshape(high, dp // high, rows, seq // rows), ("z", "y", "g", "t"))
    everything = ("z", "y", "g", "t")
    tokens = P(("z", "y"), ("g", "t"), None)
    vector = P(everything)
    matrix = P(everything, None)
    return jax.shard_map(
        body,
        mesh=split,
        in_specs=(
            tokens,
            P(("z", "y"), None),
            vector,
            vector,
            matrix,
            vector,
            matrix,
            vector,
            vector,
            vector,
            matrix,
            vector,
            matrix,
            vector,
            tokens,
        ),
        out_specs=(
            tokens,
            tokens,
            vector,
            vector,
            matrix,
            vector,
            matrix,
            vector,
            vector,
            vector,
            matrix,
            vector,
            matrix,
            vector,
        ),
        check_vma=False,
    )
```
